256 devices in a mesh: chan: 128 (over z, x, y_hi, core), tm: 2 (over y_lo).
Axes of the slice: x: 4, y: 4 (y_hi: 2, y_lo: 2; y = y_hi * 2 + y_lo), z: 8, core: 2. Of those that a mesh axis runs over, the one named last changes fastest.
Arguments:
- spectra: bfloat16 [16, 4096, 2, 2048], P('tm', 'chan'), may hold values from -74 to 74
- src_block: int32 [2], replicated, may hold values from 0 to 127
- quality: int32 [4096], P('chan'), may hold values 0 or 1
Outputs:
- stacked: float32 [32, 2, 4096, 512], P('tm', None, 'chan')
The draws below stay inside these ranges and needn't reach their ends.
All inputs are finite; a program needn't handle non-finite values. No bound on the sum of `quality` on one device may be relied on, other than what follows from the above.
Results may differ from the reference program's by a relative error of at most 0.0054.
Values may be sent and summed in bfloat16 or wider, within the bound.
A program may use at most 64 MiB of HBM per device.

```python
import math
import jax
import jax.numpy as jnp
from jax import lax

F = 2048
LAG = 512
STEPS = 2
CH_DEV = 32
W_DEV = 8
CHANNELS = 4096
WINDOWS = 16
N_CHAN = 128
N_TM = 2


def draw_spectra(key, part):
    first_key, second_key, third_key = jax.random.split(key, 3)
    base_values = jnp.clip(jax.random.normal(first_key, (WINDOWS, CHANNELS, 2, F), jnp.float32), -6.0, 6.0)
    levels = jnp.exp(jax.random.uniform(second_key, (WINDOWS, CHANNELS, 1, 1), jnp.float32, -1.5, 1.5))
    colours = jnp.exp(jax.random.uniform(third_key, (1, 1, 1, F), jnp.float32, -1.0, 1.0))
    return (base_values * levels * colours).astype(jnp.bfloat16)


def touch_ends(values, own_key, least, high):
    longest = values.shape.index(max(values.shape))
    spots = []
    for shift in (0, 1):
        where = [jax.random.randint(jax.random.fold_in(own_key, axis), (), 0, length) for axis, length in enumerate(values.shape)]
        where[longest] = (where[longest] + shift) % values.shape[longest]
        spots.append(tuple(where))
    return values.at[spots[0]].set(least).at[spots[1]].set(high)


def setup_inputs(seed: int = 0) -> dict:
    streams_of = jax.random.split(jax.random.key(seed), 4)
    return {
        "spectra": draw_spectra(jax.random.fold_in(streams_of[3], 71), 0),
        "src_block": jax.random.randint(streams_of[1], (STEPS,), 0, N_CHAN).astype(jnp.int32),
        "quality": touch_ends((jax.random.randint(streams_of[2], (CHANNELS,), 0, 10) < 9).astype(jnp.int32), jax.random.fold_in(streams_of[2], 1), 0, 1),
    }


def normalize(masked):
    mean_power = lax.optimization_barrier(jnp.mean(masked * masked, axis=(2, 3), keepdims=True))
    return (masked / jnp.sqrt(mean_power + 1e-06)).astype(jnp.bfloat16)

def lag_table(num_bins, num_lags, windows):
    freq_bins = jnp.arange(num_bins, dtype=jnp.int32)[:, None]
    shifts = jnp.arange(num_lags, dtype=jnp.int32)[None, :] - num_lags // 2
    phases = jnp.mod(freq_bins * shifts, 2 * num_bins).astype(jnp.float32) * (math.pi / num_bins)
    scaling = 1.0 / math.sqrt(2.0 * num_bins * windows)
    return jnp.concatenate([jnp.cos(phases) * scaling, -jnp.sin(phases) * scaling], 0).astype(jnp.bfloat16)

def reference(spectra, src_block, quality):
    masked = spectra.astype(jnp.float32) * quality.astype(jnp.float32)[None, :, None, None]
    whitened = normalize(masked)
    lag_weights = lag_table(F, LAG, WINDOWS).astype(jnp.float32)
    groups = whitened.reshape(N_TM, W_DEV, CHANNELS, 2, F)
    blk_size = CH_DEV * min(N_CHAN, 16)
    num_blocks = CHANNELS // blk_size
    results = []
    for step_index in range(STEPS):
        first_row = (src_block[step_index] * CH_DEV).astype(jnp.int32)
        stacked = jnp.zeros((CH_DEV, CHANNELS, LAG), jnp.float32)
        for group_index in range(N_TM):
            window_group = groups[group_index]
            source = lax.dynamic_slice_in_dim(window_group, first_row, CH_DEV, 1).astype(jnp.float32)

            def one_block(receivers):
                receivers = receivers.astype(jnp.float32)
                hp = lax.Precision.HIGHEST
                real_part = jnp.einsum('wsf,wcf->scf', source[:, :, 0], receivers[:, :, 0], precision=hp) + jnp.einsum('wsf,wcf->scf', source[:, :, 1], receivers[:, :, 1], precision=hp)
                imag_part = jnp.einsum('wsf,wcf->scf', source[:, :, 0], receivers[:, :, 1], precision=hp) - jnp.einsum('wsf,wcf->scf', source[:, :, 1], receivers[:, :, 0], precision=hp)
                cross_spec = jnp.concatenate([real_part, imag_part], -1).astype(jnp.bfloat16).astype(jnp.float32)
                return jnp.einsum('scg,gl->scl', cross_spec, lag_weights, precision=hp)
            blocked = window_group.reshape(W_DEV, num_blocks, blk_size, 2, F).transpose(1, 0, 2, 3, 4)
            mapped = lax.map(one_block, blocked)
            stacked = stacked + mapped.transpose(1, 0, 2, 3).reshape(CH_DEV, CHANNELS, LAG)
        results.append(stacked)
    return jnp.stack(results, 1)
```

```python
from functools import partial
import math

import jax
import jax.numpy as jnp
from jax import lax
from jax.experimental import pallas as pl
from jax.experimental.pallas import tpu as pltpu
from jax.sharding import PartitionSpec as P

LAG = 512
STEPS = 2


MESH = pl.DeviceIdType.MESH
GROUP = 16


def pair_even(i):
    return i + 1 - 2 * (i % 2)


def pair_odd(i, n):
    return (i + 2 * (i % 2) - 1 + n) % n


def half_even(i):
    return ((i + 1) // 2) % 2


def half_odd(i):
    return i // 2


def coords(chan):
    return chan // 16, (chan // 4) % 4, (chan // 2) % 2, chan % 2


def chan_of(z, x, y, core):
    return ((z * 4 + x) * 2 + y) * 2 + core


def spread_kernel(blk_ref, x_ref, out_ref, r1, cur1, rc, cur2, r2, cur3, rm0, rm1, *sems):
    s1s, s1r, scs, scr, s2s, s2r, sms, smr, gms, gmr, g2s, g2r, g1s, g1r, gcs, gcr = sems
    z, x, y, core = coords(lax.axis_index("chan"))
    z_even, z_odd = pair_even(z), pair_odd(z, 8)
    x_even, x_odd = pair_even(x), pair_odd(x, 4)
    z_half = z % 2
    at_xe, at_xo = chan_of(z, x_even, y, core), chan_of(z, x_odd, y, core)
    at_ze, at_zo = chan_of(z_even, x, y, core), chan_of(z_odd, x, y, core)
    at_core = chan_of(z, x, y, 1 - core)
    parts = [
        (at_xe, at_ze, half_even(x), z_half),
        (at_ze, at_xe, z_half, half_even(x)),
        (at_xo, at_zo, half_odd(x), z_half),
        (at_zo, at_xo, z_half, half_odd(x)),
    ]
    roots = [coords(blk_ref[k]) for k in range(STEPS)]
    from_xe = [r[1] == x_even for r in roots]
    from_xo = [r[1] == x_odd for r in roots]
    from_ze = [r[0] == z_even for r in roots]
    from_zo = [r[0] == z_odd for r in roots]
    from_core = [r[3] != core for r in roots]
    first_from = [from_xe, from_ze, from_xo, from_zo]
    second_from = [from_ze, from_xe, from_zo, from_xo]

    mine = [half_odd(x) * 8 + y * 4 + z // 2, half_even(x) * 8 + y * 4 + z // 2]
    peers = [[], []]
    for pair in range(2):
        for offset in range(1, GROUP):
            d_x, d_y, d_z = offset // 8, (offset // 4) % 2, offset % 4
            far_x = (x_odd, x_even)[pair] if d_x else x
            peer_z = z_half + 2 * ((z // 2 + d_z) % 4)
            peer_y = (y + d_y) % 2
            half = (half_odd(far_x), half_even(far_x))[pair]
            peers[pair].append((chan_of(peer_z, far_x, peer_y, core), half * 8 + peer_y * 4 + peer_z // 2))
    chosen = []
    for pair in range(2):
        row = []
        for r in roots:
            if pair == 0:
                row.append(half_odd(r[1]) * 8 + r[2] * 4 + r[0] // 2)
            else:
                z_in = jnp.where(r[0] % 2 == z_half, r[0] // 2, pair_odd(r[0], 8) // 2)
                row.append(half_even(r[1]) * 8 + r[2] * 4 + z_in)
        chosen.append(row)

    def send(src, dst, ssem, rsem, to):
        copy = pltpu.make_async_remote_copy(
            src_ref=src, dst_ref=dst, send_sem=ssem, recv_sem=rsem,
            device_id={"chan": to}, device_id_type=MESH,
        )
        copy.start()
        return copy

    rm = (rm0, rm1)
    barrier = pltpu.get_barrier_semaphore()
    greet = [at_ze, at_zo, at_core] + [c for c, _ in peers[0]] + [c for c, _ in peers[1][7:]]
    for to in greet:
        pl.semaphore_signal(barrier, inc=1, device_id={"chan": to}, device_id_type=MESH)
    pl.semaphore_wait(barrier, len(greet))

    pending = []
    first = []
    for p, (to, _, b1, _) in enumerate(parts):
        first.append(send(x_ref.at[p, :, 1 - b1], r1.at[p], s1s.at[p], s1r.at[p], to))
    cores = []
    for p, (_, _, b1, _) in enumerate(parts):
        first[p].wait_recv()

        @pl.loop(0, GROUP)
        def _(m):
            own, got = x_ref[p, :, b1, :, m], r1[p, :, :, m]
            for k in range(STEPS):
                cur1[k, p, :, :, m] = jnp.where(first_from[p][k], got, own)

        cores.append(send(cur1.at[:, p, 1 - core], rc.at[:, p], scs.at[p], scr.at[p], at_core))
    second = []
    for p, (_, to, _, b2) in enumerate(parts):
        cores[p].wait_recv()

        @pl.loop(0, GROUP)
        def _(m):
            for k in range(STEPS):
                cur2[k, p, :, m] = jnp.where(from_core[k], rc[k, p, :, m], cur1[k, p, core, :, m])

        second.append(send(cur2.at[:, p, 1 - b2], r2.at[:, p], s2s.at[p], s2r.at[p], to))
    group = []
    for pair in range(2):
        for p in (2 * pair, 2 * pair + 1):
            b2 = parts[p][3]
            second[p].wait_recv()

            @pl.loop(0, GROUP)
            def _(m):
                for k in range(STEPS):
                    cur3[pair, p % 2, k, m] = jnp.where(second_from[p][k], r2[k, p, m], cur2[k, p, b2, m])

        for j, (to, slot) in enumerate(peers[pair]):
            group.append(
                send(cur3.at[pair, :, :, slot], rm[pair].at[mine[pair]], sms.at[pair, j], smr.at[pair, j], to)
            )
        rm[pair][mine[pair]] = cur3[pair, :, :, mine[pair]]
    gather = []
    for pair in range(2):
        for j in range(GROUP - 1):
            group[pair * (GROUP - 1) + j].wait_recv()
        for p in (2 * pair, 2 * pair + 1):
            _, _, b1, b2 = parts[p]
            for k in range(STEPS):
                out_ref[k, p, core, b1, b2, mine[pair]] = rm[pair][chosen[pair][k], p % 2, k]
            spot = out_ref.at[:, p, core, b1, b2, mine[pair]]
            for j, (to, _) in enumerate(peers[pair]):
                gather.append(send(spot, spot, gms.at[p, j], gmr.at[p, j], to))
    back2 = []
    for p, (_, to, b1, b2) in enumerate(parts):
        for j in range(GROUP - 1):
            gather[p * (GROUP - 1) + j].wait_recv()
        spot = out_ref.at[:, p, core, b1, b2]
        back2.append(send(spot, spot, g2s.at[p], g2r.at[p], to))
    back1 = []
    for p, (to, _, b1, _) in enumerate(parts):
        back2[p].wait_recv()
        spot = out_ref.at[:, p, core, b1]
        back1.append(send(spot, spot, g1s.at[p], g1r.at[p], to))
    backc = []
    for p in range(4):
        back1[p].wait_recv()
        spot = out_ref.at[:, p, core]
        backc.append(send(spot, spot, gcs.at[p], gcr.at[p], at_core))
    for p in range(4):
        backc[p].wait_recv()
    for copy in first + cores + second + group + gather + back2 + back1 + backc:
        copy.wait_send()


def spread(block, src_block, rows=16, lanes=128):
    dma = pltpu.SemaphoreType.DMA
    vm = lambda *s: pltpu.VMEM(s + (rows, lanes), block.dtype)
    sems = []
    for shape in ((4,), (4,), (4,), (2, 15), (4, 15), (4,), (4,), (4,)):
        sems += [dma(shape), dma(shape)]
    return pl.pallas_call(
        spread_kernel,
        out_shape=jax.ShapeDtypeStruct((STEPS, 4, 2, 2, 2, GROUP, rows, lanes), block.dtype),
        in_specs=[pl.BlockSpec(memory_space=pltpu.SMEM), pl.BlockSpec(memory_space=pltpu.VMEM)],
        out_specs=pl.BlockSpec(memory_space=pltpu.VMEM),
        scratch_shapes=[
            vm(4, 2, 2, GROUP),
            vm(STEPS, 4, 2, 2, GROUP),
            vm(STEPS, 4, 2, GROUP),
            vm(STEPS, 4, 2, GROUP),
            vm(STEPS, 4, GROUP),
            vm(2, 2, STEPS, GROUP),
            vm(GROUP, 2, STEPS),
            vm(GROUP, 2, STEPS),
        ] + sems,
        compiler_params=pltpu.CompilerParams(collective_id=0, has_side_effects=True),
        name="spread",
    )(src_block, block.reshape(4, 2, 2, 2, GROUP, rows, lanes))


def normalize(masked):
    mean_power = jnp.mean(masked * masked, axis=(2, 3), keepdims=True)
    return (masked / jnp.sqrt(mean_power + 1e-06)).astype(jnp.bfloat16)


def lag_table(num_bins, num_lags, windows):
    freq_bins = jnp.arange(num_bins, dtype=jnp.int32)[:, None]
    shifts = jnp.arange(num_lags, dtype=jnp.int32)[None, :] - num_lags // 2
    phases = jnp.mod(freq_bins * shifts, 2 * num_bins).astype(jnp.float32) * (math.pi / num_bins)
    scaling = 1.0 / math.sqrt(2.0 * num_bins * windows)
    return jnp.concatenate([jnp.cos(phases) * scaling, -jnp.sin(phases) * scaling], 0).astype(
        jnp.bfloat16
    )


def block_lags(source, receivers, lag_weights):
    src_real = source[:, :, 0][:, :, None, :].astype(jnp.float32)
    src_imag = source[:, :, 1][:, :, None, :].astype(jnp.float32)
    rcv_real = receivers[:, :, 0][:, None, :, :].astype(jnp.float32)
    rcv_imag = receivers[:, :, 1][:, None, :, :].astype(jnp.float32)
    real_part = jnp.sum(src_real * rcv_real + src_imag * rcv_imag, axis=0)
    imag_part = jnp.sum(src_real * rcv_imag - src_imag * rcv_real, axis=0)
    cross_spec = jnp.concatenate([real_part, imag_part], -1).astype(jnp.bfloat16)
    return jnp.einsum("scg,gl->scl", cross_spec, lag_weights, preferred_element_type=jnp.float32)


def term_rows(source, receivers, lag_weights, first_row, row_count):
    num_windows = source.shape[0]
    num_blocks = row_count // 8
    blocked = source.reshape(num_windows, num_blocks, 8, 2, source.shape[3]).transpose(
        1, 0, 2, 3, 4
    )
    mapped = lax.map(partial(block_lags, receivers=receivers, lag_weights=lag_weights), blocked)
    return mapped.reshape(row_count, receivers.shape[1], lag_weights.shape[1])


def per_device(spectra, src_block, quality):
    num_windows = spectra.shape[0]
    channels = spectra.shape[1]
    num_bins = spectra.shape[3]
    windows = num_windows * lax.axis_size("tm")
    kept_rows = channels // lax.axis_size("tm")
    quality_mask = quality.astype(jnp.float32)[None, :, None, None]
    masked = spectra.astype(jnp.float32) * quality_mask
    receivers = normalize(masked)
    lag_weights = lag_table(num_bins, LAG, windows)
    sources = spread(receivers, src_block).reshape(STEPS, *receivers.shape)
    per_step = []
    for step_index in range(STEPS):
        term_fn = partial(term_rows, sources[step_index], receivers, lag_weights)
        per_step.append(
            lax.psum_scatter(
                term_fn(jnp.int32(0), lax.axis_size("tm") * kept_rows),
                "tm",
                scatter_dimension=0,
                tiled=True,
            )
        )
    stacked = jnp.stack(per_step, 1)
    return stacked


def solution(mesh):
    return jax.shard_map(
        per_device,
        mesh=mesh,
        in_specs=(P("tm", "chan", None, None), P(), P("chan")),
        out_specs=P("tm", None, "chan", None),
        check_vma=False,
    )
```

```python
import math

import jax
import jax.numpy as jnp
import numpy as np
from jax import lax
from jax.experimental import pallas as pl
from jax.experimental.pallas import tpu as pltpu
from jax.sharding import PartitionSpec as P

LAG = 512
STEPS = 2
WINDOWS = 16

MESH = pl.DeviceIdType.MESH
GROUP = 16


def pair_even(i):
    return i + 1 - 2 * (i % 2)


def pair_odd(i, n):
    return (i + 2 * (i % 2) - 1 + n) % n


def half_even(i):
    return ((i + 1) // 2) % 2


def half_odd(i):
    return i // 2


def coords(chan):
    return chan // 16, (chan // 4) % 4, (chan // 2) % 2, chan % 2


def chan_of(z, x, y, core):
    return ((z * 4 + x) * 2 + y) * 2 + core


def spread_kernel(blk_ref, x_ref, out_ref, r1, cur1, rc, cur2, r2, cur3, rm0, rm1, *sems):
    s1s, s1r, scs, scr, s2s, s2r, sms, smr, gms, gmr, g2s, g2r, g1s, g1r, gcs, gcr = sems
    z, x, y, core = coords(lax.axis_index("chan"))
    z_even, z_odd = pair_even(z), pair_odd(z, 8)
    x_even, x_odd = pair_even(x), pair_odd(x, 4)
    z_half = z % 2
    at_xe, at_xo = chan_of(z, x_even, y, core), chan_of(z, x_odd, y, core)
    at_ze, at_zo = chan_of(z_even, x, y, core), chan_of(z_odd, x, y, core)
    at_core = chan_of(z, x, y, 1 - core)
    parts = [
        (at_xe, at_ze, half_even(x), z_half),
        (at_ze, at_xe, z_half, half_even(x)),
        (at_xo, at_zo, half_odd(x), z_half),
        (at_zo, at_xo, z_half, half_odd(x)),
    ]
    roots = [coords(blk_ref[k]) for k in range(STEPS)]
    from_xe = [r[1] == x_even for r in roots]
    from_xo = [r[1] == x_odd for r in roots]
    from_ze = [r[0] == z_even for r in roots]
    from_zo = [r[0] == z_odd for r in roots]
    from_core = [r[3] != core for r in roots]
    first_from = [from_xe, from_ze, from_xo, from_zo]
    second_from = [from_ze, from_xe, from_zo, from_xo]

    mine = [half_odd(x) * 8 + y * 4 + z // 2, half_even(x) * 8 + y * 4 + z // 2]
    peers = [[], []]
    for pair in range(2):
        for offset in range(1, GROUP):
            d_x, d_y, d_z = offset // 8, (offset // 4) % 2, offset % 4
            far_x = (x_odd, x_even)[pair] if d_x else x
            peer_z = z_half + 2 * ((z // 2 + d_z) % 4)
            peer_y = (y + d_y) % 2
            half = (half_odd(far_x), half_even(far_x))[pair]
            peers[pair].append((chan_of(peer_z, far_x, peer_y, core), half * 8 + peer_y * 4 + peer_z // 2))
    chosen = []
    for pair in range(2):
        row = []
        for r in roots:
            if pair == 0:
                row.append(half_odd(r[1]) * 8 + r[2] * 4 + r[0] // 2)
            else:
                z_in = jnp.where(r[0] % 2 == z_half, r[0] // 2, pair_odd(r[0], 8) // 2)
                row.append(half_even(r[1]) * 8 + r[2] * 4 + z_in)
        chosen.append(row)

    def send(src, dst, ssem, rsem, to):
        copy = pltpu.make_async_remote_copy(
            src_ref=src, dst_ref=dst, send_sem=ssem, recv_sem=rsem,
            device_id={"chan": to}, device_id_type=MESH,
        )
        copy.start()
        return copy

    rm = (rm0, rm1)
    barrier = pltpu.get_barrier_semaphore()
    greet = [at_ze, at_zo, at_core] + [c for c, _ in peers[0]] + [c for c, _ in peers[1][7:]]
    for to in greet:
        pl.semaphore_signal(barrier, inc=1, device_id={"chan": to}, device_id_type=MESH)
    pl.semaphore_wait(barrier, len(greet))

    pending = []
    first = []
    for p, (to, _, b1, _) in enumerate(parts):
        first.append(send(x_ref.at[p, :, 1 - b1], r1.at[p], s1s.at[p], s1r.at[p], to))
    cores = []
    for p, (_, _, b1, _) in enumerate(parts):
        first[p].wait_recv()

        @pl.loop(0, GROUP)
        def _(m):
            own, got = x_ref[p, :, b1, :, m], r1[p, :, :, m]
            for k in range(STEPS):
                cur1[k, p, :, :, m] = jnp.where(first_from[p][k], got, own)

        cores.append(send(cur1.at[:, p, 1 - core], rc.at[:, p], scs.at[p], scr.at[p], at_core))
    second = []
    for p, (_, to, _, b2) in enumerate(parts):
        cores[p].wait_recv()

        @pl.loop(0, GROUP)
        def _(m):
            for k in range(STEPS):
                cur2[k, p, :, m] = jnp.where(from_core[k], rc[k, p, :, m], cur1[k, p, core, :, m])

        second.append(send(cur2.at[:, p, 1 - b2], r2.at[:, p], s2s.at[p], s2r.at[p], to))
    group = []
    for pair in range(2):
        for p in (2 * pair, 2 * pair + 1):
            b2 = parts[p][3]
            second[p].wait_recv()

            @pl.loop(0, GROUP)
            def _(m):
                for k in range(STEPS):
                    cur3[pair, p % 2, k, m] = jnp.where(second_from[p][k], r2[k, p, m], cur2[k, p, b2, m])

        for j, (to, slot) in enumerate(peers[pair]):
            group.append(
                send(cur3.at[pair, :, :, slot], rm[pair].at[mine[pair]], sms.at[pair, j], smr.at[pair, j], to)
            )
        rm[pair][mine[pair]] = cur3[pair, :, :, mine[pair]]
    gather = []
    for pair in range(2):
        for j in range(GROUP - 1):
            group[pair * (GROUP - 1) + j].wait_recv()
        for p in (2 * pair, 2 * pair + 1):
            _, _, b1, b2 = parts[p]
            for k in range(STEPS):
                out_ref[k, p, core, b1, b2, mine[pair]] = rm[pair][chosen[pair][k], p % 2, k]
            spot = out_ref.at[:, p, core, b1, b2, mine[pair]]
            for j, (to, _) in enumerate(peers[pair]):
                gather.append(send(spot, spot, gms.at[p, j], gmr.at[p, j], to))
    back2 = []
    for p, (_, to, b1, b2) in enumerate(parts):
        for j in range(GROUP - 1):
            gather[p * (GROUP - 1) + j].wait_recv()
        spot = out_ref.at[:, p, core, b1, b2]
        back2.append(send(spot, spot, g2s.at[p], g2r.at[p], to))
    back1 = []
    for p, (to, _, b1, _) in enumerate(parts):
        back2[p].wait_recv()
        spot = out_ref.at[:, p, core, b1]
        back1.append(send(spot, spot, g1s.at[p], g1r.at[p], to))
    backc = []
    for p in range(4):
        back1[p].wait_recv()
        spot = out_ref.at[:, p, core]
        backc.append(send(spot, spot, gcs.at[p], gcr.at[p], at_core))
    for p in range(4):
        backc[p].wait_recv()
    for copy in first + cores + second + group + gather + back2 + back1 + backc:
        copy.wait_send()


def spread(block, src_block, rows=16, lanes=128):
    dma = pltpu.SemaphoreType.DMA
    vm = lambda *s: pltpu.VMEM(s + (rows, lanes), block.dtype)
    sems = []
    for shape in ((4,), (4,), (4,), (2, 15), (4, 15), (4,), (4,), (4,)):
        sems += [dma(shape), dma(shape)]
    return pl.pallas_call(
        spread_kernel,
        out_shape=jax.ShapeDtypeStruct((STEPS, 4, 2, 2, 2, GROUP, rows, lanes), block.dtype),
        in_specs=[pl.BlockSpec(memory_space=pltpu.SMEM), pl.BlockSpec(memory_space=pltpu.VMEM)],
        out_specs=pl.BlockSpec(memory_space=pltpu.VMEM),
        scratch_shapes=[
            vm(4, 2, 2, GROUP),
            vm(STEPS, 4, 2, 2, GROUP),
            vm(STEPS, 4, 2, GROUP),
            vm(STEPS, 4, 2, GROUP),
            vm(STEPS, 4, GROUP),
            vm(2, 2, STEPS, GROUP),
            vm(GROUP, 2, STEPS),
            vm(GROUP, 2, STEPS),
        ] + sems,
        compiler_params=pltpu.CompilerParams(collective_id=0, has_side_effects=True),
        name="spread",
    )(src_block, block.reshape(4, 2, 2, 2, GROUP, rows, lanes))


def normalize(masked):
    mean_power = jnp.mean(masked * masked, axis=(2, 3), keepdims=True)
    return (masked / jnp.sqrt(mean_power + 1e-06)).astype(jnp.bfloat16)


BINS, LANES, FINE = 2048, 128, 256


def angle_tables():
    scale = 1.0 / math.sqrt(2.0 * BINS * WINDOWS)
    bins = np.arange(BINS, dtype=np.int64)[None, :]
    low = np.arange(8, dtype=np.int64)[:, None] * bins % (2 * BINS) * (math.pi / BINS)
    high = (np.arange(LAG // 8, dtype=np.int64)[:, None] * 8 - LAG // 2) * bins % (2 * BINS) * (math.pi / BINS)
    f32 = np.float32
    return (np.stack([np.cos(low), np.sin(low)]) * scale).astype(f32), np.stack([np.cos(high), np.sin(high)]).astype(f32)


def swap_matrix():
    lane = np.arange(LANES)
    swap = np.zeros((LANES, LANES), np.float32)
    imag = lane // 8 % 2
    swap[lane ^ 8, lane] = np.where(imag == 0, 1.0, -1.0)
    return swap.astype(jnp.bfloat16)


def correlate_kernel(
    own_ref, src_ref, low_ref, high_ref, swap_ref, out_ref,
    swapped, table, cross, rhs, kept, outgoing, incoming, ssem, rsem,
):
    tm = lax.axis_index("tm")
    f32, bf16 = jnp.float32, jnp.bfloat16
    barrier = pltpu.get_barrier_semaphore()
    pl.semaphore_signal(barrier, inc=1, device_id={"tm": 1 - tm}, device_id_type=MESH)
    pl.semaphore_wait(barrier, 1)

    @pl.loop(0, LAG // 16)
    def _(i):
        for part in range(BINS // 512):
            lanes = pl.ds(part * 512, 512)
            lc, ls = low_ref[0, :, lanes], low_ref[1, :, lanes]
            cos, sin = [], []
            for h in range(2):
                hc, hs = high_ref[0, pl.ds(2 * i + h, 1), lanes], high_ref[1, pl.ds(2 * i + h, 1), lanes]
                cos.append(lc * hc - ls * hs)
                sin.append(-(ls * hc + lc * hs))
            rows = pl.ds(pl.multiple_of(i * 16, 16), 16)
            table[rows, lanes] = jnp.concatenate(cos, 0).astype(bf16)
            table[rows, pl.ds(BINS + part * 512, 512)] = jnp.concatenate(sin, 0).astype(bf16)

    @pl.loop(0, 16)
    def _(i):
        chunk = own_ref[pl.ds(i * 16, 16)].reshape(512, LANES)
        swapped[pl.ds(i * 16, 16)] = (
            jnp.dot(chunk, swap_ref[...], preferred_element_type=f32).astype(bf16).reshape(16, 32, LANES)
        )

    lane2 = lax.broadcasted_iota(jnp.int32, (1, 2 * LANES), 1)
    lane1 = lax.broadcasted_iota(jnp.int32, (1, LANES), 1)
    fmask = [(lane2 % 4 == f4).astype(f32).astype(bf16) for f4 in range(4)]
    qmask = [(lane1 // 4 % 2 == q).astype(f32).astype(bf16) for q in range(2)]
    zero = jnp.zeros((64, LANES), bf16)
    mine, theirs = pl.ds(pl.multiple_of(tm * 16, 16), 16), pl.ds(pl.multiple_of((1 - tm) * 16, 16), 16)

    def one_group(g):
        real, imag = own_ref[g], swapped[g]
        pieces = [jnp.concatenate([v[:16], v[16:]], 1) for v in (real, imag)]
        lhs = jnp.concatenate([v * fmask[f4] for f4 in range(4) for v in pieces], 0)
        src = jnp.concatenate([src_ref[k, g, h] for k in range(STEPS) for h in (mine, theirs)], 0)
        rows = []
        for q in range(2):
            masked = src * qmask[q]
            rows += [jnp.concatenate([masked, zero], 1), jnp.concatenate([zero, masked], 1)]
        weights = jnp.concatenate(rows, 0)
        product = lax.dot_general(lhs, weights, (((1,), (1,)), ((), ())), preferred_element_type=f32)
        for i in range(8):
            for q in range(2):
                cross[i, q, pl.ds(pl.multiple_of(g * 16, 16), 16), :] = product[
                    16 * i : 16 * i + 16, q * LANES : (q + 1) * LANES
                ]

    @pl.loop(0, FINE // 2)
    def _(i):
        one_group(2 * i)
        one_group(2 * i + 1)

    def lag_product(pair):
        for q in range(2):
            for f4 in range(4):
                for ri in range(2):
                    first = ri * BINS + (q * 4 + f4) * FINE
                    i = f4 * 2 + ri
                    for half in range(2):
                        value = cross[i, q, pl.ds(2 * pair + half, FINE, stride=16), :]
                        rhs[pl.ds(first, FINE), pl.ds(half * LANES, LANES)] = value.astype(bf16)
        lags = jnp.dot(table[...], rhs[...], preferred_element_type=f32).T
        for half in range(2):
            for j in range(2):
                for k in range(STEPS):
                    row = ((half * 2 + j) * STEPS + k) * 32
                    spot = ((half * 2 + j) * STEPS + k) * 16
                    kept[pair, pl.ds(spot, 16)] = lags[row : row + 16]
                    outgoing[pair, pl.ds(spot, 16)] = lags[row + 16 : row + 32].astype(bf16)

    def transfer(pair):
        return pltpu.make_async_remote_copy(
            src_ref=outgoing.at[pair], dst_ref=incoming.at[pair], send_sem=ssem.at[pair], recv_sem=rsem.at[pair],
            device_id={"tm": 1 - tm}, device_id_type=MESH,
        )

    @pl.loop(0, 8)
    def _(pair):
        lag_product(pair)
        transfer(pair).start()

    @pl.loop(0, 8)
    def _(pair):
        transfer(pair).wait_recv()
        for half in range(2):
            for j in range(2):
                for k in range(STEPS):
                    spot = ((half * 2 + j) * STEPS + k) * 16
                    total = kept[pair, pl.ds(spot, 16)] + incoming[pair, pl.ds(spot, 16)].astype(f32)
                    channel = j * 16 + 2 * pair + half
                    for part in range(4):
                        row = k * 128 + channel // 8 * 32 + part * 8 + channel % 8
                        out_ref[pl.ds(row, 16, stride=256), :] = total[:, part * LANES : (part + 1) * LANES]

    @pl.loop(0, 8)
    def _(pair):
        transfer(pair).wait_send()


def correlate(own, sources):
    f32, bf16 = jnp.float32, jnp.bfloat16
    low, high = angle_tables()
    vmem = pl.BlockSpec(memory_space=pltpu.VMEM)
    return pl.pallas_call(
        correlate_kernel,
        out_shape=jax.ShapeDtypeStruct((16 * STEPS * 32 * 4, LANES), f32),
        in_specs=[vmem] * 5,
        out_specs=vmem,
        scratch_shapes=[
            pltpu.VMEM((FINE, 32, LANES), bf16),
            pltpu.VMEM((LAG, 2 * BINS), bf16),
            pltpu.VMEM((8, 2, FINE * 16, LANES), f32),
            pltpu.VMEM((2 * BINS, 2 * LANES), bf16),
            pltpu.VMEM((8, LANES, LAG), f32),
            pltpu.VMEM((8, LANES, LAG), bf16),
            pltpu.VMEM((8, LANES, LAG), bf16),
            pltpu.SemaphoreType.DMA((8,)),
            pltpu.SemaphoreType.DMA((8,)),
        ],
        compiler_params=pltpu.CompilerParams(
            collective_id=1, has_side_effects=True, vmem_limit_bytes=66_000_000
        ),
        name="correlate",
    )(own, sources, jnp.asarray(low), jnp.asarray(high), jnp.asarray(swap_matrix()))


def per_device(spectra, src_block, quality):
    quality_mask = quality.astype(jnp.float32)[None, :, None, None]
    masked = spectra.astype(jnp.float32) * quality_mask
    whitened = normalize(masked)
    block = whitened.reshape(8, 32, 2, 8, FINE).transpose(4, 1, 0, 2, 3).reshape(FINE, 32, LANES)
    block = lax.optimization_barrier(block)
    sources = spread(block, src_block).reshape(STEPS, FINE, 32, LANES)
    tiles = correlate(block, sources).reshape(16, STEPS, 4, 4, 8, LANES)
    return tiles.transpose(0, 1, 2, 4, 3, 5).reshape(16, STEPS, 32, LAG)


def solution(mesh):
    return jax.shard_map(
        per_device,
        mesh=mesh,
        in_specs=(P("tm", "chan", None, None), P(), P("chan")),
        out_specs=P("tm", None, "chan", None),
        check_vma=False,
    )
```

```python
import math

import jax
import jax.numpy as jnp
import numpy as np
from jax import lax
from jax.experimental import pallas as pl
from jax.experimental.pallas import tpu as pltpu
from jax.sharding import PartitionSpec as P

LAG = 512
STEPS = 2
WINDOWS = 16
BINS, LANES, FINE = 2048, 128, 256

MESH = pl.DeviceIdType.MESH
GROUP = 16


def pair_even(i):
    return i + 1 - 2 * (i % 2)


def pair_odd(i, n):
    return (i + 2 * (i % 2) - 1 + n) % n


def half_even(i):
    return ((i + 1) // 2) % 2


def half_odd(i):
    return i // 2


def coords(chan):
    return chan // 16, (chan // 4) % 4, (chan // 2) % 2, chan % 2


def chan_of(z, x, y, core):
    return ((z * 4 + x) * 2 + y) * 2 + core


def angle_tables():
    scale = 1.0 / math.sqrt(2.0 * BINS * WINDOWS)
    bins = np.arange(BINS, dtype=np.int64).reshape(8, 2, LANES).transpose(1, 0, 2).reshape(1, BINS)
    low = np.arange(8, dtype=np.int64)[:, None] * bins % (2 * BINS) * (math.pi / BINS)
    high = (np.arange(LAG // 8, dtype=np.int64)[:, None] * 8 - LAG // 2) * bins % (2 * BINS) * (math.pi / BINS)
    f32 = np.float32
    return (np.stack([np.cos(low), np.sin(low)]) * scale).astype(f32), np.stack([np.cos(high), np.sin(high)]).astype(f32)


def swap_matrix():
    lane = np.arange(LANES)
    swap = np.zeros((LANES, LANES), np.float32)
    imag = lane // 8 % 2
    swap[lane ^ 8, lane] = np.where(imag == 0, 1.0, -1.0)
    return swap.astype(jnp.bfloat16)


def kernel(
    blk_ref, raw_ref, quality_ref, low_ref, high_ref, swap_ref, out_ref,
    own, r1, cur1, rc, cur2, r2, cur3, rm0, rm1, src,
    swapped, table, cross, rhs, partial, kept, outgoing, incoming, *sems,
):
    s1s, s1r, scs, scr, s2s, s2r, sms, smr, gms, gmr, g2s, g2r, g1s, g1r, gcs, gcr, xs, xr = sems
    f32, bf16 = jnp.float32, jnp.bfloat16
    tm = lax.axis_index("tm")
    z, x, y, core = coords(lax.axis_index("chan"))
    z_even, z_odd = pair_even(z), pair_odd(z, 8)
    x_even, x_odd = pair_even(x), pair_odd(x, 4)
    z_half = z % 2
    at_xe, at_xo = chan_of(z, x_even, y, core), chan_of(z, x_odd, y, core)
    at_ze, at_zo = chan_of(z_even, x, y, core), chan_of(z_odd, x, y, core)
    at_core = chan_of(z, x, y, 1 - core)
    parts = [
        (at_xe, at_ze, half_even(x), z_half),
        (at_ze, at_xe, z_half, half_even(x)),
        (at_xo, at_zo, half_odd(x), z_half),
        (at_zo, at_xo, z_half, half_odd(x)),
    ]
    mine = [half_odd(x) * 8 + y * 4 + z // 2, half_even(x) * 8 + y * 4 + z // 2]
    peers = [[], []]
    for pair in range(2):
        for offset in range(1, GROUP):
            d_x, d_y, d_z = offset // 8, (offset // 4) % 2, offset % 4
            far_x = (x_odd, x_even)[pair] if d_x else x
            peer_z = z_half + 2 * ((z // 2 + d_z) % 4)
            peer_y = (y + d_y) % 2
            half = (half_odd(far_x), half_even(far_x))[pair]
            peers[pair].append((chan_of(peer_z, far_x, peer_y, core), half * 8 + peer_y * 4 + peer_z // 2))

    barrier = pltpu.get_barrier_semaphore()
    greet = [at_ze, at_zo, at_core] + [c for c, _ in peers[0]] + [c for c, _ in peers[1][7:]]
    for to in greet:
        pl.semaphore_signal(barrier, inc=1, device_id={"chan": to}, device_id_type=MESH)
    pl.semaphore_signal(barrier, inc=1, device_id={"tm": 1 - tm}, device_id_type=MESH)

    @pl.loop(0, 32)
    def _(c):
        value = raw_ref[:, c].astype(f32).reshape(LANES, FINE).T
        for p in range(4):
            cross[p // 2, p % 2, pl.ds(c, 64, stride=32), :] = value[64 * p : 64 * p + 64]

    def add_power(i, total):
        for p in range(4):
            for u in range(4):
                v = cross[p // 2, p % 2, pl.ds(pl.multiple_of(i * 128 + u * 32, 32), 32), :]
                total = total + v * v
        return total

    power = lax.fori_loop(0, 16, add_power, jnp.zeros((32, LANES), f32))
    lane1 = lax.broadcasted_iota(jnp.int32, (32, LANES), 1)
    for shift in (1, 2, 4, 8):
        other = jnp.where(lane1 // shift % 2 == 0, pltpu.roll(power, LANES - shift, 1), pltpu.roll(power, shift, 1))
        power = power + other
    usable = quality_ref[...].astype(f32)
    scale = usable / jnp.sqrt(power * (usable * usable) / (2.0 * BINS) + 1e-06)
    for p in range(4):

        @pl.loop(0, 8)
        def _(i):
            for u in range(8):
                v = cross[p // 2, p % 2, pl.ds(pl.multiple_of(i * 256 + u * 32, 32), 32), :] * scale
                for j in range(2):
                    own[p, i // 4, i // 2 % 2, i % 2, 2 * u + j] = v[16 * j : 16 * j + 16].astype(bf16)

    pl.semaphore_wait(barrier, len(greet) + 1)

    roots = [coords(blk_ref[k]) for k in range(STEPS)]
    from_xe = [r[1] == x_even for r in roots]
    from_xo = [r[1] == x_odd for r in roots]
    from_ze = [r[0] == z_even for r in roots]
    from_zo = [r[0] == z_odd for r in roots]
    from_core = [r[3] != core for r in roots]
    first_from = [from_xe, from_ze, from_xo, from_zo]
    second_from = [from_ze, from_xe, from_zo, from_xo]
    chosen = []
    for pair in range(2):
        row = []
        for r in roots:
            if pair == 0:
                row.append(half_odd(r[1]) * 8 + r[2] * 4 + r[0] // 2)
            else:
                z_in = jnp.where(r[0] % 2 == z_half, r[0] // 2, pair_odd(r[0], 8) // 2)
                row.append(half_even(r[1]) * 8 + r[2] * 4 + z_in)
        chosen.append(row)
    rm = (rm0, rm1)

    def send(src_ref, dst_ref, ssem, rsem, to):
        copy = pltpu.make_async_remote_copy(
            src_ref=src_ref, dst_ref=dst_ref, send_sem=ssem, recv_sem=rsem,
            device_id={"chan": to}, device_id_type=MESH,
        )
        copy.start()
        return copy

    first = []
    for p, (to, _, b1, _) in enumerate(parts):
        first.append(send(own.at[p, :, 1 - b1], r1.at[p], s1s.at[p], s1r.at[p], to))

    @pl.loop(0, LAG // 16)
    def _(i):
        for part in range(BINS // 512):
            lanes = pl.ds(part * 512, 512)
            lc, ls = low_ref[0, :, lanes], low_ref[1, :, lanes]
            cos, sin = [], []
            for h in range(2):
                hc, hs = high_ref[0, pl.ds(2 * i + h, 1), lanes], high_ref[1, pl.ds(2 * i + h, 1), lanes]
                cos.append(lc * hc - ls * hs)
                sin.append(-(ls * hc + lc * hs))
            rows = pl.ds(pl.multiple_of(i * 16, 16), 16)
            pair, within = part // 2, part % 2 * 512
            table[pair, rows, pl.ds(within, 512)] = jnp.concatenate(cos, 0).astype(bf16)
            table[pair, rows, pl.ds(1024 + within, 512)] = jnp.concatenate(sin, 0).astype(bf16)

    for p in range(4):

        @pl.loop(0, 8)
        def _(i):
            chunk = own[p, i // 4, i // 2 % 2, i % 2].reshape(256, LANES)
            swapped[8 * p + i] = (
                jnp.dot(chunk, swap_ref[...], preferred_element_type=f32).astype(bf16).reshape(GROUP, 16, LANES)
            )

    cores = []
    for p, (_, _, b1, _) in enumerate(parts):
        first[p].wait_recv()

        @pl.loop(0, GROUP)
        def _(m):
            held, got = own[p, :, b1, :, m], r1[p, :, :, m]
            for k in range(STEPS):
                cur1[k, p, :, :, m] = jnp.where(first_from[p][k], got, held)

        cores.append(send(cur1.at[:, p, 1 - core], rc.at[:, p], scs.at[p], scr.at[p], at_core))
    second = []
    for p, (_, to, _, b2) in enumerate(parts):
        cores[p].wait_recv()

        @pl.loop(0, GROUP)
        def _(m):
            for k in range(STEPS):
                cur2[k, p, :, m] = jnp.where(from_core[k], rc[k, p, :, m], cur1[k, p, core, :, m])

        second.append(send(cur2.at[:, p, 1 - b2], r2.at[:, p], s2s.at[p], s2r.at[p], to))
    group = []
    for pair in range(2):
        for p in (2 * pair, 2 * pair + 1):
            b2 = parts[p][3]
            second[p].wait_recv()

            @pl.loop(0, GROUP)
            def _(m):
                for k in range(STEPS):
                    cur3[pair, p % 2, k, m] = jnp.where(second_from[p][k], r2[k, p, m], cur2[k, p, b2, m])

        for j, (to, slot) in enumerate(peers[pair]):
            group.append(
                send(cur3.at[pair, :, :, slot], rm[pair].at[mine[pair]], sms.at[pair, j], smr.at[pair, j], to)
            )
        rm[pair][mine[pair]] = cur3[pair, :, :, mine[pair]]

    def spot(p, level):
        _, _, b1, b2 = parts[p]
        if level == 0:
            return src.at[:, pl.ds((((p * 2 + core) * 2 + b1) * 2 + b2) * 16 + mine[p // 2], 1)]
        if level == 1:
            return src.at[:, pl.ds((((p * 2 + core) * 2 + b1) * 2 + b2) * 16, 16)]
        if level == 2:
            return src.at[:, pl.ds(((p * 2 + core) * 2 + b1) * 32, 32)]
        return src.at[:, pl.ds((p * 2 + core) * 64, 64)]

    gather, back2, back1, backc = [[], [], [], []], [None] * 4, [None] * 4, [None] * 4

    def start_gather(pair):
        for j in range(GROUP - 1):
            group[pair * (GROUP - 1) + j].wait_recv()
        for p in (2 * pair, 2 * pair + 1):
            _, _, b1, b2 = parts[p]
            at = (((p * 2 + core) * 2 + b1) * 2 + b2) * 16 + mine[pair]
            for k in range(STEPS):
                src[k, at] = rm[pair][chosen[pair][k], p % 2, k]
            for j, (to, _) in enumerate(peers[pair]):
                gather[p].append(send(spot(p, 0), spot(p, 0), gms.at[p, j], gmr.at[p, j], to))

    def start_back2(pair):
        for p in (2 * pair, 2 * pair + 1):
            for copy in gather[p]:
                copy.wait_recv()
            back2[p] = send(spot(p, 1), spot(p, 1), g2s.at[p], g2r.at[p], parts[p][1])

    def start_back1(pair):
        for p in (2 * pair, 2 * pair + 1):
            back2[p].wait_recv()
            back1[p] = send(spot(p, 2), spot(p, 2), g1s.at[p], g1r.at[p], parts[p][0])

    def start_core(pair):
        for p in (2 * pair, 2 * pair + 1):
            back1[p].wait_recv()
            backc[p] = send(spot(p, 3), spot(p, 3), gcs.at[p], gcr.at[p], at_core)

    lane2 = lax.broadcasted_iota(jnp.int32, (1, 2 * LANES), 1)
    lane0 = lax.broadcasted_iota(jnp.int32, (1, LANES), 1)
    fmask = [(lane2 % 4 == f4).astype(f32).astype(bf16) for f4 in range(4)]
    qmask = [(lane0 // 4 % 2 == q).astype(f32).astype(bf16) for q in range(2)]
    zero = jnp.zeros((64, LANES), bf16)

    def products(p):
        @pl.loop(0, 8)
        def _(i):
            for u in range(8):
                real = [own[p, i // 4, i // 2 % 2, i % 2, 2 * u + j] for j in range(2)]
                imag = [swapped[8 * p + i, 2 * u + j] for j in range(2)]
                pieces = [jnp.concatenate(v, 1) for v in (real, imag)]
                lhs = jnp.concatenate([v * fmask[f4] for f4 in range(4) for v in pieces], 0)
                at = p * 128 + i * 16 + 2 * u
                sources = jnp.concatenate([src[k, at + h] for k in range(STEPS) for h in (tm, 1 - tm)], 0)
                rows = []
                for q in range(2):
                    masked = sources * qmask[q]
                    rows += [jnp.concatenate([masked, zero], 1), jnp.concatenate([zero, masked], 1)]
                weights = jnp.concatenate(rows, 0)
                product = lax.dot_general(lhs, weights, (((1,), (1,)), ((), ())), preferred_element_type=f32)
                row = pl.multiple_of((p % 2 * 64 + i * 8 + u) * 16, 16)
                for n in range(8):
                    for q in range(2):
                        cross[n, q, pl.ds(row, 16), :] = product[16 * n : 16 * n + 16, q * LANES : (q + 1) * LANES]

    def lag_sums(pair, cols):
        for q in range(2):
            for f4 in range(4):
                for ri in range(2):
                    for half in range(2):
                        value = cross[f4 * 2 + ri, q, pl.ds(2 * cols + half, LANES, stride=16), :]
                        rows = pl.ds(ri * 1024 + (q * 4 + f4) * LANES, LANES)
                        rhs[rows, pl.ds(half * LANES, LANES)] = value.astype(bf16)
        return jnp.dot(table[pair], rhs[...], preferred_element_type=f32)

    def transfer(cols):
        return pltpu.make_async_remote_copy(
            src_ref=outgoing.at[cols], dst_ref=incoming.at[cols], send_sem=xs.at[cols], recv_sem=xr.at[cols],
            device_id={"tm": 1 - tm}, device_id_type=MESH,
        )

    start_gather(0)
    start_gather(1)
    start_back2(0)
    start_back1(0)
    start_back2(1)
    start_core(0)
    start_back1(1)
    backc[0].wait_recv()
    products(0)
    start_core(1)
    backc[1].wait_recv()
    products(1)

    @pl.loop(0, 8)
    def _(cols):
        partial[cols] = lag_sums(0, cols)

    backc[2].wait_recv()
    products(2)
    backc[3].wait_recv()
    products(3)

    @pl.loop(0, 8)
    def _(cols):
        lags = (partial[cols] + lag_sums(1, cols)).T
        for n in range(8):
            kept[cols, pl.ds(n * 16, 16)] = lags[n * 32 : n * 32 + 16]
            outgoing[cols, pl.ds(n * 16, 16)] = lags[n * 32 + 16 : n * 32 + 32].astype(bf16)
        transfer(cols).start()

    @pl.loop(0, 8)
    def _(cols):
        transfer(cols).wait_recv()
        for half in range(2):
            for j in range(2):
                for k in range(STEPS):
                    at = pl.ds(((half * 2 + j) * STEPS + k) * 16, 16)
                    total = kept[cols, at] + incoming[cols, at].astype(f32)
                    channel = j * 16 + 2 * cols + half
                    for part in range(4):
                        row = k * 128 + channel // 8 * 32 + part * 8 + channel % 8
                        out_ref[pl.ds(row, 16, stride=256), :] = total[:, part * LANES : (part + 1) * LANES]

    @pl.loop(0, 8)
    def _(cols):
        transfer(cols).wait_send()

    for copy in first + cores + second + group + gather[0] + gather[1] + gather[2] + gather[3] + back2 + back1 + backc:
        copy.wait_send()


def per_device(spectra, src_block, quality):
    f32, bf16 = jnp.float32, jnp.bfloat16
    raw = spectra.reshape(8, 32, 2, 8, FINE)
    low, high = angle_tables()
    vmem = pl.BlockSpec(memory_space=pltpu.VMEM)
    dma = pltpu.SemaphoreType.DMA
    rows = lambda *s: pltpu.VMEM(s + (16, LANES), bf16)
    sems = []
    for shape in ((4,), (4,), (4,), (2, 15), (4, 15), (4,), (4,), (4,), (8,)):
        sems += [dma(shape), dma(shape)]
    tiles = pl.pallas_call(
        kernel,
        out_shape=jax.ShapeDtypeStruct((16 * STEPS * 32 * 4, LANES), f32),
        in_specs=[pl.BlockSpec(memory_space=pltpu.SMEM)] + [vmem] * 5,
        out_specs=vmem,
        scratch_shapes=[
            rows(4, 2, 2, 2, GROUP),
            rows(4, 2, 2, GROUP),
            rows(STEPS, 4, 2, 2, GROUP),
            rows(STEPS, 4, 2, GROUP),
            rows(STEPS, 4, 2, GROUP),
            rows(STEPS, 4, GROUP),
            rows(2, 2, STEPS, GROUP),
            rows(GROUP, 2, STEPS),
            rows(GROUP, 2, STEPS),
            rows(STEPS, 512),
            rows(32, GROUP),
            pltpu.VMEM((2, LAG, BINS), bf16),
            pltpu.VMEM((8, 2, 128 * 16, LANES), f32),
            pltpu.VMEM((BINS, 2 * LANES), bf16),
            pltpu.VMEM((8, LAG, 2 * LANES), f32),
            pltpu.VMEM((8, LANES, LAG), f32),
            pltpu.VMEM((8, LANES, LAG), bf16),
            pltpu.VMEM((8, LANES, LAG), bf16),
        ]
        + sems,
        compiler_params=pltpu.CompilerParams(collective_id=0, has_side_effects=True, vmem_limit_bytes=66_000_000),
        name="correlate",
    )(src_block, raw, quality.reshape(32, 1), jnp.asarray(low), jnp.asarray(high), jnp.asarray(swap_matrix()))
    tiles = tiles.reshape(16, STEPS, 4, 4, 8, LANES)
    return tiles.transpose(0, 1, 2, 4, 3, 5).reshape(16, STEPS, 32, LAG)


def solution(mesh):
    return jax.shard_map(
        per_device,
        mesh=mesh,
        in_specs=(P("tm", "chan", None, None), P(), P("chan")),
        out_specs=P("tm", None, "chan", None),
        check_vma=False,
    )
```

```python
import math

import jax
import jax.numpy as jnp
import numpy as np
from jax import lax
from jax.experimental import pallas as pl
from jax.experimental.pallas import tpu as pltpu
from jax.sharding import PartitionSpec as P

LAG = 512
STEPS = 2
WINDOWS = 16
BINS, LANES, FINE = 2048, 128, 256

MESH = pl.DeviceIdType.MESH
GROUP = 16


def pair_even(i):
    return i + 1 - 2 * (i % 2)


def pair_odd(i, n):
    return (i + 2 * (i % 2) - 1 + n) % n


def half_even(i):
    return ((i + 1) // 2) % 2


def half_odd(i):
    return i // 2


def coords(chan):
    return chan // 16, (chan // 4) % 4, (chan // 2) % 2, chan % 2


def chan_of(z, x, y, core):
    return ((z * 4 + x) * 2 + y) * 2 + core


def angle_tables():
    scale = 1.0 / math.sqrt(2.0 * BINS * WINDOWS)
    bins = np.arange(BINS, dtype=np.int64)[None, :]
    low = np.arange(8, dtype=np.int64)[:, None] * bins % (2 * BINS) * (math.pi / BINS)
    high = (np.arange(LAG // 8, dtype=np.int64)[:, None] * 8 - LAG // 2) * bins % (2 * BINS) * (math.pi / BINS)
    f32 = np.float32
    return (np.stack([np.cos(low), np.sin(low)]) * scale).astype(f32), np.stack([np.cos(high), np.sin(high)]).astype(f32)


def swap_matrix():
    lane = np.arange(LANES)
    swap = np.zeros((LANES, LANES), np.float32)
    imag = lane // 8 % 2
    swap[lane ^ 8, lane] = np.where(imag == 0, 1.0, -1.0)
    return swap.astype(jnp.bfloat16)


def kernel(
    blk_ref, raw_ref, quality_ref, low_ref, high_ref, swap_ref, out_ref,
    own, r1, cur1, rc, cur2, r2, cur3, rm00, rm01, rm10, rm11, src,
    swapped, table, cross, rhs, kept, outgoing, incoming, *sems,
):
    s1s, s1r, scs, scr, s2s, s2r, sms, smr, gms, gmr, g2s, g2r, g1s, g1r, gcs, gcr, xs, xr = sems
    f32, bf16 = jnp.float32, jnp.bfloat16
    tm = lax.axis_index("tm")
    z, x, y, core = coords(lax.axis_index("chan"))
    z_even, z_odd = pair_even(z), pair_odd(z, 8)
    x_even, x_odd = pair_even(x), pair_odd(x, 4)
    z_half = z % 2
    at_xe, at_xo = chan_of(z, x_even, y, core), chan_of(z, x_odd, y, core)
    at_ze, at_zo = chan_of(z_even, x, y, core), chan_of(z_odd, x, y, core)
    at_core = chan_of(z, x, y, 1 - core)
    parts = [
        (at_xe, at_ze, half_even(x), z_half),
        (at_ze, at_xe, z_half, half_even(x)),
        (at_xo, at_zo, half_odd(x), z_half),
        (at_zo, at_xo, z_half, half_odd(x)),
    ]
    mine = [half_odd(x) * 8 + y * 4 + z // 2, half_even(x) * 8 + y * 4 + z // 2]
    peers = [[], []]
    for pair in range(2):
        for offset in range(1, GROUP):
            d_x, d_y, d_z = offset // 8, (offset // 4) % 2, offset % 4
            far_x = (x_odd, x_even)[pair] if d_x else x
            peer_z = z_half + 2 * ((z // 2 + d_z) % 4)
            peer_y = (y + d_y) % 2
            half = (half_odd(far_x), half_even(far_x))[pair]
            peers[pair].append((chan_of(peer_z, far_x, peer_y, core), half * 8 + peer_y * 4 + peer_z // 2))

    barrier = pltpu.get_barrier_semaphore()
    greet = [at_ze, at_zo, at_core] + [c for c, _ in peers[0]] + [c for c, _ in peers[1][7:]]
    for to in greet:
        pl.semaphore_signal(barrier, inc=1, device_id={"chan": to}, device_id_type=MESH)
    pl.semaphore_signal(barrier, inc=1, device_id={"tm": 1 - tm}, device_id_type=MESH)

    @pl.loop(0, 32)
    def _(c):
        value = raw_ref[:, c].astype(f32).reshape(LANES, FINE).T * quality_ref[c].astype(f32)
        for p in range(4):
            cross[p // 2, p % 2, pl.ds(c, 64, stride=32), :] = value[64 * p : 64 * p + 64]

    def add_power(i, total):
        for p in range(4):
            for u in range(4):
                v = cross[p // 2, p % 2, pl.ds(pl.multiple_of(i * 128 + u * 32, 32), 32), :]
                total = total + v * v
        return total

    power = lax.fori_loop(0, 16, add_power, jnp.zeros((32, LANES), f32))
    lane1 = lax.broadcasted_iota(jnp.int32, (32, LANES), 1)
    for shift in (1, 2, 4, 8):
        other = jnp.where(lane1 // shift % 2 == 0, pltpu.roll(power, LANES - shift, 1), pltpu.roll(power, shift, 1))
        power = power + other
    scale = 1.0 / jnp.sqrt(power / (2.0 * BINS) + 1e-06)
    for p in range(4):

        @pl.loop(0, 8)
        def _(i):
            for u in range(8):
                v = cross[p // 2, p % 2, pl.ds(pl.multiple_of(i * 256 + u * 32, 32), 32), :] * scale
                for j in range(2):
                    own[p, i // 4, i // 2 % 2, i % 2, 2 * u + j] = v[16 * j : 16 * j + 16].astype(bf16)

    pl.semaphore_wait(barrier, len(greet) + 1)

    roots = [coords(blk_ref[k]) for k in range(STEPS)]
    from_xe = [r[1] == x_even for r in roots]
    from_xo = [r[1] == x_odd for r in roots]
    from_ze = [r[0] == z_even for r in roots]
    from_zo = [r[0] == z_odd for r in roots]
    from_core = [r[3] != core for r in roots]
    first_from = [from_xe, from_ze, from_xo, from_zo]
    second_from = [from_ze, from_xe, from_zo, from_xo]
    chosen = []
    for pair in range(2):
        row = []
        for r in roots:
            if pair == 0:
                row.append(half_odd(r[1]) * 8 + r[2] * 4 + r[0] // 2)
            else:
                z_in = jnp.where(r[0] % 2 == z_half, r[0] // 2, pair_odd(r[0], 8) // 2)
                row.append(half_even(r[1]) * 8 + r[2] * 4 + z_in)
        chosen.append(row)
    rm = ((rm00, rm01), (rm10, rm11))

    def send(src_ref, dst_ref, ssem, rsem, to):
        copy = pltpu.make_async_remote_copy(
            src_ref=src_ref, dst_ref=dst_ref, send_sem=ssem, recv_sem=rsem,
            device_id={"chan": to}, device_id_type=MESH,
        )
        copy.start()
        return copy

    first = []
    for p, (to, _, b1, _) in enumerate(parts):
        first.append(send(own.at[p, :, 1 - b1], r1.at[p], s1s.at[p], s1r.at[p], to))

    @pl.loop(0, LAG // 16)
    def _(i):
        for part in range(BINS // 512):
            lanes = pl.ds(part * 512, 512)
            lc, ls = low_ref[0, :, lanes], low_ref[1, :, lanes]
            cos, sin = [], []
            for h in range(2):
                hc, hs = high_ref[0, pl.ds(2 * i + h, 1), lanes], high_ref[1, pl.ds(2 * i + h, 1), lanes]
                cos.append(lc * hc - ls * hs)
                sin.append(-(ls * hc + lc * hs))
            rows = pl.ds(pl.multiple_of(i * 16, 16), 16)
            table[rows, lanes] = jnp.concatenate(cos, 0).astype(bf16)
            table[rows, pl.ds(BINS + part * 512, 512)] = jnp.concatenate(sin, 0).astype(bf16)

    for p in range(4):

        @pl.loop(0, 8)
        def _(i):
            chunk = own[p, i // 4, i // 2 % 2, i % 2].reshape(256, LANES)
            swapped[8 * p + i] = (
                jnp.dot(chunk, swap_ref[...], preferred_element_type=f32).astype(bf16).reshape(GROUP, 16, LANES)
            )

    cores, second, group, gather, back2, back1, backc = ([[None] * 4 for _ in range(STEPS)] for _ in range(7))

    def start_core_stage(p):
        _, _, b1, _ = parts[p]
        first[p].wait_recv()

        @pl.loop(0, GROUP)
        def _(m):
            held, got = own[p, :, b1, :, m], r1[p, :, :, m]
            for k in range(STEPS):
                cur1[k, p, :, :, m] = jnp.where(first_from[p][k], got, held)

        for k in range(STEPS):
            cores[k][p] = send(cur1.at[k, p, 1 - core], rc.at[k, p], scs.at[k, p], scr.at[k, p], at_core)

    def start_second(k, p):
        _, to, _, b2 = parts[p]
        cores[k][p].wait_recv()

        @pl.loop(0, GROUP)
        def _(m):
            cur2[k, p, :, m] = jnp.where(from_core[k], rc[k, p, :, m], cur1[k, p, core, :, m])

        second[k][p] = send(cur2.at[k, p, 1 - b2], r2.at[k, p], s2s.at[k, p], s2r.at[k, p], to)

    def take_second(k, p):
        b2 = parts[p][3]
        second[k][p].wait_recv()

        @pl.loop(0, GROUP)
        def _(m):
            cur3[p // 2, p % 2, k, m] = jnp.where(second_from[p][k], r2[k, p, m], cur2[k, p, b2, m])

    def start_group(k):
        for pair in range(2):
            at = mine[pair]
            group[k][pair] = [
                send(cur3.at[pair, :, k, slot], rm[pair][k].at[at], sms.at[k, pair, j], smr.at[k, pair, j], to)
                for j, (to, slot) in enumerate(peers[pair])
            ]
            rm[pair][k][at] = cur3[pair, :, k, at]

    def spot(k, p, level):
        _, _, b1, b2 = parts[p]
        if level == 0:
            return src.at[k, pl.ds((((p * 2 + core) * 2 + b1) * 2 + b2) * 16 + mine[p // 2], 1)]
        if level == 1:
            return src.at[k, pl.ds((((p * 2 + core) * 2 + b1) * 2 + b2) * 16, 16)]
        if level == 2:
            return src.at[k, pl.ds(((p * 2 + core) * 2 + b1) * 32, 32)]
        return src.at[k, pl.ds((p * 2 + core) * 64, 64)]

    def start_gather(k):
        for pair in range(2):
            for copy in group[k][pair]:
                copy.wait_recv()
            for p in (2 * pair, 2 * pair + 1):
                _, _, b1, b2 = parts[p]
                at = (((p * 2 + core) * 2 + b1) * 2 + b2) * 16 + mine[pair]
                src[k, at] = rm[pair][k][chosen[pair][k], p % 2]
                gather[k][p] = [
                    send(spot(k, p, 0), spot(k, p, 0), gms.at[k, p, j], gmr.at[k, p, j], to)
                    for j, (to, _) in enumerate(peers[pair])
                ]

    def start_back2(k):
        for p in range(4):
            for copy in gather[k][p]:
                copy.wait_recv()
            back2[k][p] = send(spot(k, p, 1), spot(k, p, 1), g2s.at[k, p], g2r.at[k, p], parts[p][1])

    def start_back1(k):
        for p in range(4):
            back2[k][p].wait_recv()
            back1[k][p] = send(spot(k, p, 2), spot(k, p, 2), g1s.at[k, p], g1r.at[k, p], parts[p][0])

    def start_core(k):
        for p in range(4):
            back1[k][p].wait_recv()
            backc[k][p] = send(spot(k, p, 3), spot(k, p, 3), gcs.at[k, p], gcr.at[k, p], at_core)

    lane2 = lax.broadcasted_iota(jnp.int32, (1, 2 * LANES), 1)
    lane0 = lax.broadcasted_iota(jnp.int32, (1, LANES), 1)
    fmask = [(lane2 % 4 == f4).astype(f32).astype(bf16) for f4 in range(4)]
    qmask = [(lane0 // 4 % 2 == q).astype(f32).astype(bf16) for q in range(2)]
    zero = jnp.zeros((32, LANES), bf16)
    low_lane = lax.broadcasted_iota(jnp.int32, (8, LANES), 1) < 64

    def products(k, p):
        backc[k][p].wait_recv()

        @pl.loop(0, 8)
        def _(i):
            for u in range(8):
                real = [own[p, i // 4, i // 2 % 2, i % 2, 2 * u + j] for j in range(2)]
                imag = [swapped[8 * p + i, 2 * u + j] for j in range(2)]
                pieces = [jnp.concatenate(v, 1) for v in (real, imag)]
                lhs = jnp.concatenate([v * fmask[f4] for f4 in range(4) for v in pieces], 0)
                at = p * 128 + i * 16 + 2 * u
                sources = jnp.concatenate([src[k, at + h] for h in (tm, 1 - tm)], 0)
                rows = []
                for q in range(2):
                    masked = sources * qmask[q]
                    rows += [jnp.concatenate([masked, zero], 1), jnp.concatenate([zero, masked], 1)]
                weights = jnp.concatenate(rows, 0)
                product = lax.dot_general(lhs, weights, (((1,), (1,)), ((), ())), preferred_element_type=f32)
                row = pl.multiple_of((p * 64 + i * 8 + u) * 8, 8)
                for n in range(8):
                    upper, lower = product[16 * n : 16 * n + 8], product[16 * n + 8 : 16 * n + 16]
                    cross[n, 0, pl.ds(row, 8), :] = jnp.where(low_lane, upper, pltpu.roll(lower, 64, 1))
                    cross[n, 1, pl.ds(row, 8), :] = jnp.where(low_lane, pltpu.roll(upper, 64, 1), lower)

    def transfer(at):
        return pltpu.make_async_remote_copy(
            src_ref=outgoing.at[at], dst_ref=incoming.at[at], send_sem=xs.at[at], recv_sem=xr.at[at],
            device_id={"tm": 1 - tm}, device_id_type=MESH,
        )

    def lags(k):
        @pl.loop(0, 4)
        def _(cols):
            for q in range(2):
                for f4 in range(4):
                    for ri in range(2):
                        for half in range(2):
                            value = cross[f4 * 2 + ri, q, pl.ds(2 * cols + half, FINE, stride=8), :]
                            rows = pl.ds(ri * BINS + (q * 4 + f4) * FINE, FINE)
                            rhs[rows, pl.ds(half * LANES, LANES)] = value.astype(bf16)
            sums = jnp.dot(table[...], rhs[...], preferred_element_type=f32).T
            at = k * 4 + cols
            for n in range(8):
                kept[at, pl.ds(n * 16, 16)] = sums[n * 32 : n * 32 + 16]
                outgoing[at, pl.ds(n * 16, 16)] = sums[n * 32 + 16 : n * 32 + 32].astype(bf16)
            transfer(at).start()

    def finish(k):
        @pl.loop(0, 4)
        def _(cols):
            at = k * 4 + cols
            transfer(at).wait_recv()
            for half in range(2):
                for h in range(2):
                    for j in range(2):
                        spot16 = pl.ds(((half * 2 + h) * 2 + j) * 16, 16)
                        total = kept[at, spot16] + incoming[at, spot16].astype(f32)
                        channel = 2 * cols + half
                        for part in range(4):
                            row = k * 128 + (j * 2 + h) * 32 + part * 8 + channel
                            out_ref[pl.ds(row, 16, stride=256), :] = total[:, part * LANES : (part + 1) * LANES]

    for p in range(4):
        start_core_stage(p)
    for k in range(STEPS):
        for p in range(4):
            start_second(k, p)
    for p in range(4):
        take_second(0, p)
    start_group(0)
    for p in range(4):
        take_second(1, p)
    start_gather(0)
    start_group(1)
    start_back2(0)
    start_back1(0)
    start_gather(1)
    start_core(0)
    products(0, 0)
    start_back2(1)
    products(0, 1)
    start_back1(1)
    products(0, 2)
    start_core(1)
    products(0, 3)
    lags(0)
    for p in range(4):
        products(1, p)
    lags(1)
    finish(0)
    finish(1)

    @pl.loop(0, 8)
    def _(at):
        transfer(at).wait_send()

    for copy in first:
        copy.wait_send()
    for k in range(STEPS):
        for copy in cores[k] + second[k] + back2[k] + back1[k] + backc[k] + sum(gather[k], []) + group[k][0] + group[k][1]:
            copy.wait_send()


def per_device(spectra, src_block, quality):
    f32, bf16 = jnp.float32, jnp.bfloat16
    raw = spectra.reshape(8, 32, 2, 8, FINE)
    low, high = angle_tables()
    vmem, smem = (pl.BlockSpec(memory_space=space) for space in (pltpu.VMEM, pltpu.SMEM))
    dma = pltpu.SemaphoreType.DMA
    rows = lambda *s: pltpu.VMEM(s + (16, LANES), bf16)
    sems = []
    for shape in ((4,), (2, 4), (2, 4), (2, 2, 15), (2, 4, 15), (2, 4), (2, 4), (2, 4), (8,)):
        sems += [dma(shape), dma(shape)]
    tiles = pl.pallas_call(
        kernel,
        out_shape=jax.ShapeDtypeStruct((16 * STEPS * 32 * 4, LANES), f32),
        in_specs=[smem, vmem, smem] + [vmem] * 3,
        out_specs=vmem,
        scratch_shapes=[
            rows(4, 2, 2, 2, GROUP),
            rows(4, 2, 2, GROUP),
            rows(STEPS, 4, 2, 2, GROUP),
            rows(STEPS, 4, 2, GROUP),
            rows(STEPS, 4, 2, GROUP),
            rows(STEPS, 4, GROUP),
            rows(2, 2, STEPS, GROUP),
            rows(GROUP, 2),
            rows(GROUP, 2),
            rows(GROUP, 2),
            rows(GROUP, 2),
            rows(STEPS, 512),
            rows(32, GROUP),
            pltpu.VMEM((LAG, 2 * BINS), bf16),
            pltpu.VMEM((8, 2, FINE * 8, LANES), f32),
            pltpu.VMEM((2 * BINS, 2 * LANES), bf16),
            pltpu.VMEM((8, LANES, LAG), f32),
            pltpu.VMEM((8, LANES, LAG), bf16),
            pltpu.VMEM((8, LANES, LAG), bf16),
        ]
        + sems,
        compiler_params=pltpu.CompilerParams(collective_id=0, has_side_effects=True, vmem_limit_bytes=66_000_000),
        name="correlate",
    )(src_block, raw, quality, jnp.asarray(low), jnp.asarray(high), jnp.asarray(swap_matrix()))
    tiles = tiles.reshape(16, STEPS, 4, 4, 8, LANES)
    return tiles.transpose(0, 1, 2, 4, 3, 5).reshape(16, STEPS, 32, LAG)


def solution(mesh):
    return jax.shard_map(
        per_device,
        mesh=mesh,
        in_specs=(P("tm", "chan", None, None), P(), P("chan")),
        out_specs=P("tm", None, "chan", None),
        check_vma=False,
    )
```

```python
import math

import jax
import jax.numpy as jnp
import numpy as np
from jax import lax
from jax.experimental import pallas as pl
from jax.experimental.pallas import tpu as pltpu
from jax.sharding import PartitionSpec as P

LAG = 512
STEPS = 2
WINDOWS = 16
BINS, LANES, FINE = 2048, 128, 256
HALF_ROWS = LAG // 2 + 16

MESH = pl.DeviceIdType.MESH
GROUP = 16


def pair_even(i):
    return i + 1 - 2 * (i % 2)


def pair_odd(i, n):
    return (i + 2 * (i % 2) - 1 + n) % n


def half_even(i):
    return ((i + 1) // 2) % 2


def half_odd(i):
    return i // 2


def coords(chan):
    return chan // 16, (chan // 4) % 4, (chan // 2) % 2, chan % 2


def chan_of(z, x, y, core):
    return ((z * 4 + x) * 2 + y) * 2 + core


def angle_tables():
    scale = 1.0 / math.sqrt(2.0 * BINS * WINDOWS)
    bins = np.arange(BINS, dtype=np.int64)[None, :]
    low = np.arange(8, dtype=np.int64)[:, None] * bins % (2 * BINS) * (math.pi / BINS)
    high = np.arange(0, HALF_ROWS, 8, dtype=np.int64)[:, None] * bins % (2 * BINS) * (math.pi / BINS)
    f32 = np.float32
    return (np.stack([np.cos(low), np.sin(low)]) * scale).astype(f32), np.stack([np.cos(high), np.sin(high)]).astype(f32)


def swap_matrix():
    lane = np.arange(LANES)
    swap = np.zeros((LANES, LANES), np.float32)
    imag = lane // 8 % 2
    swap[lane ^ 8, lane] = np.where(imag == 0, 1.0, -1.0)
    return swap.astype(jnp.bfloat16)


def kernel(
    blk_ref, raw_ref, quality_ref, low_ref, high_ref, swap_ref, out_ref,
    own, r1, cur1, rc, cur2, r2, cur3, rm00, rm01, rm10, rm11, src,
    swapped, table, cross, rhs, kept, outgoing, incoming, *sems,
):
    s1s, s1r, scs, scr, s2s, s2r, sms, smr, gms, gmr, g2s, g2r, g1s, g1r, gcs, gcr, xs, xr = sems
    f32, bf16 = jnp.float32, jnp.bfloat16
    tm = lax.axis_index("tm")
    z, x, y, core = coords(lax.axis_index("chan"))
    z_even, z_odd = pair_even(z), pair_odd(z, 8)
    x_even, x_odd = pair_even(x), pair_odd(x, 4)
    z_half = z % 2
    at_xe, at_xo = chan_of(z, x_even, y, core), chan_of(z, x_odd, y, core)
    at_ze, at_zo = chan_of(z_even, x, y, core), chan_of(z_odd, x, y, core)
    at_core = chan_of(z, x, y, 1 - core)
    parts = [
        (at_xe, at_ze, half_even(x), z_half),
        (at_ze, at_xe, z_half, half_even(x)),
        (at_xo, at_zo, half_odd(x), z_half),
        (at_zo, at_xo, z_half, half_odd(x)),
    ]
    mine = [half_odd(x) * 8 + y * 4 + z // 2, half_even(x) * 8 + y * 4 + z // 2]
    peers = [[], []]
    for pair in range(2):
        for offset in range(1, GROUP):
            d_x, d_y, d_z = offset // 8, (offset // 4) % 2, offset % 4
            far_x = (x_odd, x_even)[pair] if d_x else x
            peer_z = z_half + 2 * ((z // 2 + d_z) % 4)
            peer_y = (y + d_y) % 2
            half = (half_odd(far_x), half_even(far_x))[pair]
            peers[pair].append((chan_of(peer_z, far_x, peer_y, core), half * 8 + peer_y * 4 + peer_z // 2))

    barrier = pltpu.get_barrier_semaphore()
    greet = [at_ze, at_zo, at_core] + [c for c, _ in peers[0]] + [c for c, _ in peers[1][7:]]
    for to in greet:
        pl.semaphore_signal(barrier, inc=1, device_id={"chan": to}, device_id_type=MESH)
    pl.semaphore_signal(barrier, inc=1, device_id={"tm": 1 - tm}, device_id_type=MESH)

    @pl.loop(0, 32)
    def _(c):
        value = raw_ref[:, c].astype(f32).reshape(LANES, FINE).T * quality_ref[c].astype(f32)
        for p in range(4):
            cross[p // 2, p % 2, pl.ds(c, 64, stride=32), :] = value[64 * p : 64 * p + 64]

    def add_power(i, total):
        for p in range(4):
            for u in range(4):
                v = cross[p // 2, p % 2, pl.ds(pl.multiple_of(i * 128 + u * 32, 32), 32), :]
                total = total + v * v
        return total

    power = lax.fori_loop(0, 16, add_power, jnp.zeros((32, LANES), f32))
    lane1 = lax.broadcasted_iota(jnp.int32, (32, LANES), 1)
    for shift in (1, 2, 4, 8):
        other = jnp.where(lane1 // shift % 2 == 0, pltpu.roll(power, LANES - shift, 1), pltpu.roll(power, shift, 1))
        power = power + other
    scale = 1.0 / jnp.sqrt(power / (2.0 * BINS) + 1e-06)
    for p in range(4):

        @pl.loop(0, 8)
        def _(i):
            for u in range(8):
                v = cross[p // 2, p % 2, pl.ds(pl.multiple_of(i * 256 + u * 32, 32), 32), :] * scale
                for j in range(2):
                    own[p, i // 4, i // 2 % 2, i % 2, 2 * u + j] = v[16 * j : 16 * j + 16].astype(bf16)

    pl.semaphore_wait(barrier, len(greet) + 1)

    roots = [coords(blk_ref[k]) for k in range(STEPS)]
    from_xe = [r[1] == x_even for r in roots]
    from_xo = [r[1] == x_odd for r in roots]
    from_ze = [r[0] == z_even for r in roots]
    from_zo = [r[0] == z_odd for r in roots]
    from_core = [r[3] != core for r in roots]
    first_from = [from_xe, from_ze, from_xo, from_zo]
    second_from = [from_ze, from_xe, from_zo, from_xo]
    chosen = []
    for pair in range(2):
        row = []
        for r in roots:
            if pair == 0:
                row.append(half_odd(r[1]) * 8 + r[2] * 4 + r[0] // 2)
            else:
                z_in = jnp.where(r[0] % 2 == z_half, r[0] // 2, pair_odd(r[0], 8) // 2)
                row.append(half_even(r[1]) * 8 + r[2] * 4 + z_in)
        chosen.append(row)
    rm = ((rm00, rm01), (rm10, rm11))

    def send(src_ref, dst_ref, ssem, rsem, to):
        copy = pltpu.make_async_remote_copy(
            src_ref=src_ref, dst_ref=dst_ref, send_sem=ssem, recv_sem=rsem,
            device_id={"chan": to}, device_id_type=MESH,
        )
        copy.start()
        return copy

    first = []
    for p, (to, _, b1, _) in enumerate(parts):
        first.append(send(own.at[p, :, 1 - b1], r1.at[p], s1s.at[p], s1r.at[p], to))

    @pl.loop(0, HALF_ROWS // 16)
    def _(i):
        for part in range(BINS // 512):
            lanes = pl.ds(part * 512, 512)
            lc, ls = low_ref[0, :, lanes], low_ref[1, :, lanes]
            cos, sin = [], []
            for h in range(2):
                hc, hs = high_ref[0, pl.ds(2 * i + h, 1), lanes], high_ref[1, pl.ds(2 * i + h, 1), lanes]
                cos.append(lc * hc - ls * hs)
                sin.append(-(ls * hc + lc * hs))
            rows = pl.ds(pl.multiple_of(i * 16, 16), 16)
            table[rows, lanes] = jnp.concatenate(cos, 0).astype(bf16)
            table[rows, pl.ds(BINS + part * 512, 512)] = jnp.concatenate(sin, 0).astype(bf16)

    for p in range(4):

        @pl.loop(0, 8)
        def _(i):
            chunk = own[p, i // 4, i // 2 % 2, i % 2].reshape(256, LANES)
            swapped[8 * p + i] = (
                jnp.dot(chunk, swap_ref[...], preferred_element_type=f32).astype(bf16).reshape(GROUP, 16, LANES)
            )

    cores, second, group, gather, back2, back1, backc = ([[None] * 4 for _ in range(STEPS)] for _ in range(7))

    def start_core_stage(p):
        _, _, b1, _ = parts[p]
        first[p].wait_recv()

        @pl.loop(0, GROUP)
        def _(m):
            held, got = own[p, :, b1, :, m], r1[p, :, :, m]
            for k in range(STEPS):
                cur1[k, p, :, :, m] = jnp.where(first_from[p][k], got, held)

        for k in range(STEPS):
            cores[k][p] = send(cur1.at[k, p, 1 - core], rc.at[k, p], scs.at[k, p], scr.at[k, p], at_core)

    def start_second(k, p):
        _, to, _, b2 = parts[p]
        cores[k][p].wait_recv()

        @pl.loop(0, GROUP)
        def _(m):
            cur2[k, p, :, m] = jnp.where(from_core[k], rc[k, p, :, m], cur1[k, p, core, :, m])

        second[k][p] = send(cur2.at[k, p, 1 - b2], r2.at[k, p], s2s.at[k, p], s2r.at[k, p], to)

    def take_second(k, p):
        b2 = parts[p][3]
        second[k][p].wait_recv()

        @pl.loop(0, GROUP)
        def _(m):
            cur3[p // 2, p % 2, k, m] = jnp.where(second_from[p][k], r2[k, p, m], cur2[k, p, b2, m])

    def start_group(k):
        for pair in range(2):
            at = mine[pair]
            group[k][pair] = [
                send(cur3.at[pair, :, k, slot], rm[pair][k].at[at], sms.at[k, pair, j], smr.at[k, pair, j], to)
                for j, (to, slot) in enumerate(peers[pair])
            ]
            rm[pair][k][at] = cur3[pair, :, k, at]

    def spot(k, p, level):
        _, _, b1, b2 = parts[p]
        if level == 0:
            return src.at[k, pl.ds((((p * 2 + core) * 2 + b1) * 2 + b2) * 16 + mine[p // 2], 1)]
        if level == 1:
            return src.at[k, pl.ds((((p * 2 + core) * 2 + b1) * 2 + b2) * 16, 16)]
        if level == 2:
            return src.at[k, pl.ds(((p * 2 + core) * 2 + b1) * 32, 32)]
        return src.at[k, pl.ds((p * 2 + core) * 64, 64)]

    def start_gather(k):
        for pair in range(2):
            for copy in group[k][pair]:
                copy.wait_recv()
            for p in (2 * pair, 2 * pair + 1):
                _, _, b1, b2 = parts[p]
                at = (((p * 2 + core) * 2 + b1) * 2 + b2) * 16 + mine[pair]
                src[k, at] = rm[pair][k][chosen[pair][k], p % 2]
                gather[k][p] = [
                    send(spot(k, p, 0), spot(k, p, 0), gms.at[k, p, j], gmr.at[k, p, j], to)
                    for j, (to, _) in enumerate(peers[pair])
                ]

    def start_back2(k):
        for p in range(4):
            for copy in gather[k][p]:
                copy.wait_recv()
            back2[k][p] = send(spot(k, p, 1), spot(k, p, 1), g2s.at[k, p], g2r.at[k, p], parts[p][1])

    def start_back1(k):
        for p in range(4):
            back2[k][p].wait_recv()
            back1[k][p] = send(spot(k, p, 2), spot(k, p, 2), g1s.at[k, p], g1r.at[k, p], parts[p][0])

    def start_core(k):
        for p in range(4):
            back1[k][p].wait_recv()
            backc[k][p] = send(spot(k, p, 3), spot(k, p, 3), gcs.at[k, p], gcr.at[k, p], at_core)

    lane2 = lax.broadcasted_iota(jnp.int32, (1, 2 * LANES), 1)
    lane0 = lax.broadcasted_iota(jnp.int32, (1, LANES), 1)
    fmask = [(lane2 % 4 == f4).astype(f32).astype(bf16) for f4 in range(4)]
    qmask = [(lane0 // 4 % 2 == q).astype(f32).astype(bf16) for q in range(2)]
    zero = jnp.zeros((32, LANES), bf16)
    low_lane = lax.broadcasted_iota(jnp.int32, (8, LANES), 1) < 64

    def products(k, p):
        backc[k][p].wait_recv()

        @pl.loop(0, 8)
        def _(i):
            for u in range(8):
                real = [own[p, i // 4, i // 2 % 2, i % 2, 2 * u + j] for j in range(2)]
                imag = [swapped[8 * p + i, 2 * u + j] for j in range(2)]
                pieces = [jnp.concatenate(v, 1) for v in (real, imag)]
                lhs = jnp.concatenate([v * fmask[f4] for f4 in range(4) for v in pieces], 0)
                at = p * 128 + i * 16 + 2 * u
                sources = jnp.concatenate([src[k, at + h] for h in (tm, 1 - tm)], 0)
                rows = []
                for q in range(2):
                    masked = sources * qmask[q]
                    rows += [jnp.concatenate([masked, zero], 1), jnp.concatenate([zero, masked], 1)]
                weights = jnp.concatenate(rows, 0)
                product = lax.dot_general(lhs, weights, (((1,), (1,)), ((), ())), preferred_element_type=f32)
                row = pl.multiple_of((p * 64 + i * 8 + u) * 8, 8)
                for n in range(8):
                    upper, lower = product[16 * n : 16 * n + 8], product[16 * n + 8 : 16 * n + 16]
                    cross[n, 0, pl.ds(row, 8), :] = jnp.where(low_lane, upper, pltpu.roll(lower, 64, 1))
                    cross[n, 1, pl.ds(row, 8), :] = jnp.where(low_lane, pltpu.roll(upper, 64, 1), lower)

    def transfer(at):
        return pltpu.make_async_remote_copy(
            src_ref=outgoing.at[at], dst_ref=incoming.at[at], send_sem=xs.at[at], recv_sem=xr.at[at],
            device_id={"tm": 1 - tm}, device_id_type=MESH,
        )

    lane3 = lax.broadcasted_iota(jnp.int32, (FINE, LANES), 1)
    lane_zero, mirrored = lane3 == 0, (LANES - lane3) % LANES

    def mirror(value):
        return jnp.take_along_axis(value, mirrored, axis=1, mode="promise_in_bounds")

    def lags(k):
        @pl.loop(0, 4)
        def _(cols):
            for q in range(2):
                for f4 in range(4):
                    for ri in range(2):
                        for half in range(2):
                            value = cross[f4 * 2 + ri, q, pl.ds(2 * cols + half, FINE, stride=8), :]
                            rows = pl.ds(ri * BINS + (q * 4 + f4) * FINE, FINE)
                            rhs[rows, pl.ds(half * LANES, LANES)] = value.astype(bf16)
            even = jnp.dot(table[:, :BINS], rhs[:BINS], preferred_element_type=f32)
            odd = jnp.dot(table[:, BINS:], rhs[BINS:], preferred_element_type=f32)
            right, left = (even + odd)[:FINE].T, (even - odd)[:FINE].T
            farthest = (even - odd)[FINE : FINE + 8].T[:, :1]
            near, far = (mirror(left[:, at : at + LANES]) for at in (0, LANES))
            sums = jnp.concatenate([jnp.where(lane_zero, farthest, far), jnp.where(lane_zero, far, near), right], 1)
            at = k * 4 + cols
            for n in range(8):
                kept[at, pl.ds(n * 16, 16)] = sums[n * 32 : n * 32 + 16]
                outgoing[at, pl.ds(n * 16, 16)] = sums[n * 32 + 16 : n * 32 + 32].astype(bf16)
            transfer(at).start()

    def finish(k):
        @pl.loop(0, 4)
        def _(cols):
            at = k * 4 + cols
            transfer(at).wait_recv()
            for half in range(2):
                for h in range(2):
                    for j in range(2):
                        spot16 = pl.ds(((half * 2 + h) * 2 + j) * 16, 16)
                        total = kept[at, spot16] + incoming[at, spot16].astype(f32)
                        channel = 2 * cols + half
                        for part in range(4):
                            row = k * 128 + (j * 2 + h) * 32 + part * 8 + channel
                            out_ref[pl.ds(row, 16, stride=256), :] = total[:, part * LANES : (part + 1) * LANES]

    for p in range(4):
        start_core_stage(p)
    for k in range(STEPS):
        for p in range(4):
            start_second(k, p)
    for p in range(4):
        take_second(0, p)
    start_group(0)
    for p in range(4):
        take_second(1, p)
    start_gather(0)
    start_group(1)
    start_back2(0)
    start_back1(0)
    start_gather(1)
    start_core(0)
    products(0, 0)
    start_back2(1)
    products(0, 1)
    start_back1(1)
    products(0, 2)
    start_core(1)
    products(0, 3)
    lags(0)
    for p in range(4):
        products(1, p)
    lags(1)
    finish(0)
    finish(1)

    @pl.loop(0, 8)
    def _(at):
        transfer(at).wait_send()

    for copy in first:
        copy.wait_send()
    for k in range(STEPS):
        for copy in cores[k] + second[k] + back2[k] + back1[k] + backc[k] + sum(gather[k], []) + group[k][0] + group[k][1]:
            copy.wait_send()


def per_device(spectra, src_block, quality):
    f32, bf16 = jnp.float32, jnp.bfloat16
    raw = spectra.reshape(8, 32, 2, 8, FINE)
    low, high = angle_tables()
    vmem, smem = (pl.BlockSpec(memory_space=space) for space in (pltpu.VMEM, pltpu.SMEM))
    dma = pltpu.SemaphoreType.DMA
    rows = lambda *s: pltpu.VMEM(s + (16, LANES), bf16)
    sems = []
    for shape in ((4,), (2, 4), (2, 4), (2, 2, 15), (2, 4, 15), (2, 4), (2, 4), (2, 4), (8,)):
        sems += [dma(shape), dma(shape)]
    tiles = pl.pallas_call(
        kernel,
        out_shape=jax.ShapeDtypeStruct((16 * STEPS * 32 * 4, LANES), f32),
        in_specs=[smem, vmem, smem] + [vmem] * 3,
        out_specs=vmem,
        scratch_shapes=[
            rows(4, 2, 2, 2, GROUP),
            rows(4, 2, 2, GROUP),
            rows(STEPS, 4, 2, 2, GROUP),
            rows(STEPS, 4, 2, GROUP),
            rows(STEPS, 4, 2, GROUP),
            rows(STEPS, 4, GROUP),
            rows(2, 2, STEPS, GROUP),
            rows(GROUP, 2),
            rows(GROUP, 2),
            rows(GROUP, 2),
            rows(GROUP, 2),
            rows(STEPS, 512),
            rows(32, GROUP),
            pltpu.VMEM((HALF_ROWS, 2 * BINS), bf16),
            pltpu.VMEM((8, 2, FINE * 8, LANES), f32),
            pltpu.VMEM((2 * BINS, 2 * LANES), bf16),
            pltpu.VMEM((8, LANES, LAG), f32),
            pltpu.VMEM((8, LANES, LAG), bf16),
            pltpu.VMEM((8, LANES, LAG), bf16),
        ]
        + sems,
        compiler_params=pltpu.CompilerParams(collective_id=0, has_side_effects=True, vmem_limit_bytes=66_000_000),
        name="correlate",
    )(src_block, raw, quality, jnp.asarray(low), jnp.asarray(high), jnp.asarray(swap_matrix()))
    tiles = tiles.reshape(16, STEPS, 4, 4, 8, LANES)
    return tiles.transpose(0, 1, 2, 4, 3, 5).reshape(16, STEPS, 32, LAG)


def solution(mesh):
    return jax.shard_map(
        per_device,
        mesh=mesh,
        in_specs=(P("tm", "chan", None, None), P(), P("chan")),
        out_specs=P("tm", None, "chan", None),
        check_vma=False,
    )
```

```python
import math

import jax
import jax.numpy as jnp
import numpy as np
from jax import lax
from jax.experimental import pallas as pl
from jax.experimental.pallas import tpu as pltpu
from jax.sharding import PartitionSpec as P

LAG = 512
STEPS = 2
WINDOWS = 16
BINS, LANES, FINE = 2048, 128, 256
HALF_ROWS = LAG // 2 + 16

MESH = pl.DeviceIdType.MESH
GROUP = 16


def pair_even(i):
    return i + 1 - 2 * (i % 2)


def pair_odd(i, n):
    return (i + 2 * (i % 2) - 1 + n) % n


def half_even(i):
    return ((i + 1) // 2) % 2


def half_odd(i):
    return i // 2


def coords(chan):
    return chan // 16, (chan // 4) % 4, (chan // 2) % 2, chan % 2


def chan_of(z, x, y, core):
    return ((z * 4 + x) * 2 + y) * 2 + core


def angle_tables():
    scale = 1.0 / math.sqrt(2.0 * BINS * WINDOWS)
    bins = np.arange(BINS, dtype=np.int64)[None, :]
    low = np.arange(8, dtype=np.int64)[:, None] * bins % (2 * BINS) * (math.pi / BINS)
    high = np.arange(0, HALF_ROWS, 8, dtype=np.int64)[:, None] * bins % (2 * BINS) * (math.pi / BINS)
    f32 = np.float32
    return (np.stack([np.cos(low), np.sin(low)]) * scale).astype(f32), np.stack([np.cos(high), np.sin(high)]).astype(f32)


def swap_matrix():
    lane = np.arange(LANES)
    swap = np.zeros((LANES, LANES), np.float32)
    imag = lane // 8 % 2
    swap[lane ^ 8, lane] = np.where(imag == 0, 1.0, -1.0)
    return swap.astype(jnp.bfloat16)


def kernel(
    blk_ref, raw_ref, quality_ref, low_ref, high_ref, swap_ref, out_ref,
    own, r1, cur1, rc, cur2, r2, cur3, rm00, rm01, rm10, rm11, src,
    swapped, table, cross, rhs, kept, outgoing, incoming, *sems,
):
    s1s, s1r, scs, scr, s2s, s2r, sms, smr, gms, gmr, g2s, g2r, g1s, g1r, gcs, gcr, xs, xr = sems
    f32, bf16 = jnp.float32, jnp.bfloat16
    tm = lax.axis_index("tm")
    z, x, y, core = coords(lax.axis_index("chan"))
    z_even, z_odd = pair_even(z), pair_odd(z, 8)
    x_even, x_odd = pair_even(x), pair_odd(x, 4)
    z_half = z % 2
    at_xe, at_xo = chan_of(z, x_even, y, core), chan_of(z, x_odd, y, core)
    at_ze, at_zo = chan_of(z_even, x, y, core), chan_of(z_odd, x, y, core)
    at_core = chan_of(z, x, y, 1 - core)
    parts = [
        (at_xe, at_ze, half_even(x), z_half),
        (at_ze, at_xe, z_half, half_even(x)),
        (at_xo, at_zo, half_odd(x), z_half),
        (at_zo, at_xo, z_half, half_odd(x)),
    ]
    mine = [half_odd(x) * 8 + y * 4 + z // 2, half_even(x) * 8 + y * 4 + z // 2]
    peers = [[], []]
    for pair in range(2):
        for offset in range(1, GROUP):
            d_x, d_y, d_z = offset // 8, (offset // 4) % 2, offset % 4
            far_x = (x_odd, x_even)[pair] if d_x else x
            peer_z = z_half + 2 * ((z // 2 + d_z) % 4)
            peer_y = (y + d_y) % 2
            half = (half_odd(far_x), half_even(far_x))[pair]
            peers[pair].append((chan_of(peer_z, far_x, peer_y, core), half * 8 + peer_y * 4 + peer_z // 2))

    barrier = pltpu.get_barrier_semaphore()
    greet = [at_ze, at_zo, at_core] + [c for c, _ in peers[0]] + [c for c, _ in peers[1][7:]]
    for to in greet:
        pl.semaphore_signal(barrier, inc=1, device_id={"chan": to}, device_id_type=MESH)
    pl.semaphore_signal(barrier, inc=1, device_id={"tm": 1 - tm}, device_id_type=MESH)

    @pl.loop(0, 32)
    def _(c):
        value = raw_ref[:, c].astype(f32).reshape(LANES, FINE).T * quality_ref[c].astype(f32)
        for p in range(4):
            cross[p // 2, p % 2, pl.ds(c, 64, stride=32), :] = value[64 * p : 64 * p + 64]

    def add_power(i, total):
        for p in range(4):
            for u in range(4):
                v = cross[p // 2, p % 2, pl.ds(pl.multiple_of(i * 128 + u * 32, 32), 32), :]
                total = total + v * v
        return total

    power = lax.fori_loop(0, 16, add_power, jnp.zeros((32, LANES), f32))
    lane1 = lax.broadcasted_iota(jnp.int32, (32, LANES), 1)
    for shift in (1, 2, 4, 8):
        other = jnp.where(lane1 // shift % 2 == 0, pltpu.roll(power, LANES - shift, 1), pltpu.roll(power, shift, 1))
        power = power + other
    scale = 1.0 / jnp.sqrt(power / (2.0 * BINS) + 1e-06)
    for p in range(4):

        @pl.loop(0, 8)
        def _(i):
            for u in range(8):
                v = cross[p // 2, p % 2, pl.ds(pl.multiple_of(i * 256 + u * 32, 32), 32), :] * scale
                for j in range(2):
                    own[p, i // 4, i // 2 % 2, i % 2, 2 * u + j] = v[16 * j : 16 * j + 16].astype(bf16)

    pl.semaphore_wait(barrier, len(greet) + 1)

    roots = [coords(blk_ref[k]) for k in range(STEPS)]
    from_xe = [r[1] == x_even for r in roots]
    from_xo = [r[1] == x_odd for r in roots]
    from_ze = [r[0] == z_even for r in roots]
    from_zo = [r[0] == z_odd for r in roots]
    from_core = [r[3] != core for r in roots]
    first_from = [from_xe, from_ze, from_xo, from_zo]
    second_from = [from_ze, from_xe, from_zo, from_xo]
    chosen = []
    for pair in range(2):
        row = []
        for r in roots:
            if pair == 0:
                row.append(half_odd(r[1]) * 8 + r[2] * 4 + r[0] // 2)
            else:
                z_in = jnp.where(r[0] % 2 == z_half, r[0] // 2, pair_odd(r[0], 8) // 2)
                row.append(half_even(r[1]) * 8 + r[2] * 4 + z_in)
        chosen.append(row)
    rm = ((rm00, rm01), (rm10, rm11))

    def send(src_ref, dst_ref, ssem, rsem, to):
        copy = pltpu.make_async_remote_copy(
            src_ref=src_ref, dst_ref=dst_ref, send_sem=ssem, recv_sem=rsem,
            device_id={"chan": to}, device_id_type=MESH,
        )
        copy.start()
        return copy

    first = []
    for p, (to, _, b1, _) in enumerate(parts):
        first.append(send(own.at[p, :, 1 - b1], r1.at[p], s1s.at[p], s1r.at[p], to))

    @pl.loop(0, HALF_ROWS // 16)
    def _(i):
        for part in range(BINS // 512):
            lanes = pl.ds(part * 512, 512)
            lc, ls = low_ref[0, :, lanes], low_ref[1, :, lanes]
            cos, sin = [], []
            for h in range(2):
                hc, hs = high_ref[0, pl.ds(2 * i + h, 1), lanes], high_ref[1, pl.ds(2 * i + h, 1), lanes]
                cos.append(lc * hc - ls * hs)
                sin.append(-(ls * hc + lc * hs))
            rows = pl.ds(pl.multiple_of(i * 16, 16), 16)
            table[rows, lanes] = jnp.concatenate(cos, 0).astype(bf16)
            table[rows, pl.ds(BINS + part * 512, 512)] = jnp.concatenate(sin, 0).astype(bf16)

    for p in range(4):

        @pl.loop(0, 8)
        def _(i):
            chunk = own[p, i // 4, i // 2 % 2, i % 2].reshape(256, LANES)
            swapped[8 * p + i] = (
                jnp.dot(chunk, swap_ref[...], preferred_element_type=f32).astype(bf16).reshape(GROUP, 16, LANES)
            )

    cores, second, group, gather, back2, back1, backc = ([[None] * 4 for _ in range(STEPS)] for _ in range(7))

    def start_core_stage(p):
        _, _, b1, _ = parts[p]
        first[p].wait_recv()

        @pl.loop(0, GROUP)
        def _(m):
            held, got = own[p, :, b1, :, m], r1[p, :, :, m]
            for k in range(STEPS):
                cur1[k, p, :, :, m] = jnp.where(first_from[p][k], got, held)

        for k in range(STEPS):
            cores[k][p] = send(cur1.at[k, p, 1 - core], rc.at[k, p], scs.at[k, p], scr.at[k, p], at_core)

    def start_second(k, p):
        _, to, _, b2 = parts[p]
        cores[k][p].wait_recv()

        @pl.loop(0, GROUP)
        def _(m):
            cur2[k, p, :, m] = jnp.where(from_core[k], rc[k, p, :, m], cur1[k, p, core, :, m])

        second[k][p] = send(cur2.at[k, p, 1 - b2], r2.at[k, p], s2s.at[k, p], s2r.at[k, p], to)

    def take_second(k, p):
        b2 = parts[p][3]
        second[k][p].wait_recv()

        @pl.loop(0, GROUP)
        def _(m):
            cur3[p // 2, p % 2, k, m] = jnp.where(second_from[p][k], r2[k, p, m], cur2[k, p, b2, m])

    def start_group(k):
        for pair in range(2):
            at = mine[pair]
            group[k][pair] = [
                send(cur3.at[pair, :, k, slot], rm[pair][k].at[at], sms.at[k, pair, j], smr.at[k, pair, j], to)
                for j, (to, slot) in enumerate(peers[pair])
            ]
            rm[pair][k][at] = cur3[pair, :, k, at]

    def spot(k, p, level):
        _, _, b1, b2 = parts[p]
        if level == 0:
            return src.at[k, pl.ds((((p * 2 + core) * 2 + b1) * 2 + b2) * 16 + mine[p // 2], 1)]
        if level == 1:
            return src.at[k, pl.ds((((p * 2 + core) * 2 + b1) * 2 + b2) * 16, 16)]
        if level == 2:
            return src.at[k, pl.ds(((p * 2 + core) * 2 + b1) * 32, 32)]
        return src.at[k, pl.ds((p * 2 + core) * 64, 64)]

    def start_gather(k):
        for pair in range(2):
            for copy in group[k][pair]:
                copy.wait_recv()
            for p in (2 * pair, 2 * pair + 1):
                _, _, b1, b2 = parts[p]
                at = (((p * 2 + core) * 2 + b1) * 2 + b2) * 16 + mine[pair]
                src[k, at] = rm[pair][k][chosen[pair][k], p % 2]
                gather[k][p] = [
                    send(spot(k, p, 0), spot(k, p, 0), gms.at[k, p, j], gmr.at[k, p, j], to)
                    for j, (to, _) in enumerate(peers[pair])
                ]

    def start_back2(k):
        for p in range(4):
            for copy in gather[k][p]:
                copy.wait_recv()
            back2[k][p] = send(spot(k, p, 1), spot(k, p, 1), g2s.at[k, p], g2r.at[k, p], parts[p][1])

    def start_back1(k):
        for p in range(4):
            back2[k][p].wait_recv()
            back1[k][p] = send(spot(k, p, 2), spot(k, p, 2), g1s.at[k, p], g1r.at[k, p], parts[p][0])

    def start_core(k):
        for p in range(4):
            back1[k][p].wait_recv()
            backc[k][p] = send(spot(k, p, 3), spot(k, p, 3), gcs.at[k, p], gcr.at[k, p], at_core)

    lane2 = lax.broadcasted_iota(jnp.int32, (1, 2 * LANES), 1)
    lane0 = lax.broadcasted_iota(jnp.int32, (1, LANES), 1)
    fmask = [(lane2 % 4 == f4).astype(f32).astype(bf16) for f4 in range(4)]
    qmask = [(lane0 // 4 % 2 == q).astype(f32).astype(bf16) for q in range(2)]
    zero = jnp.zeros((32, LANES), bf16)
    low_lane = lax.broadcasted_iota(jnp.int32, (8, LANES), 1) < 64

    def products(k, p):
        backc[k][p].wait_recv()

        @pl.loop(0, 4)
        def _(half_i):
            for uu in range(16):
                i, u = half_i * 2 + uu // 8, uu % 8
                real = [own[p, half_i // 2, half_i % 2, uu // 8, 2 * u + j] for j in range(2)]
                imag = [swapped[8 * p + i, 2 * u + j] for j in range(2)]
                pieces = [jnp.concatenate(v, 1) for v in (real, imag)]
                lhs = jnp.concatenate([v * fmask[f4] for f4 in range(4) for v in pieces], 0)
                at = p * 128 + i * 16 + 2 * u
                sources = jnp.concatenate([src[k, at + h] for h in (tm, 1 - tm)], 0)
                rows = []
                for q in range(2):
                    masked = sources * qmask[q]
                    rows += [jnp.concatenate([masked, zero], 1), jnp.concatenate([zero, masked], 1)]
                weights = jnp.concatenate(rows, 0)
                product = lax.dot_general(lhs, weights, (((1,), (1,)), ((), ())), preferred_element_type=f32)
                row = pl.multiple_of((p * 64 + i * 8 + u) * 8, 8)
                for n in range(8):
                    upper, lower = product[16 * n : 16 * n + 8], product[16 * n + 8 : 16 * n + 16]
                    cross[n, 0, pl.ds(row, 8), :] = jnp.where(low_lane, upper, pltpu.roll(lower, 64, 1))
                    cross[n, 1, pl.ds(row, 8), :] = jnp.where(low_lane, pltpu.roll(upper, 64, 1), lower)

    def transfer(at):
        return pltpu.make_async_remote_copy(
            src_ref=outgoing.at[at], dst_ref=incoming.at[at], send_sem=xs.at[at], recv_sem=xr.at[at],
            device_id={"tm": 1 - tm}, device_id_type=MESH,
        )

    lane3 = lax.broadcasted_iota(jnp.int32, (FINE, LANES), 1)
    lane_zero, mirrored = lane3 == 0, (LANES - lane3) % LANES

    def mirror(value):
        return jnp.take_along_axis(value, mirrored, axis=1, mode="promise_in_bounds")

    def lags(k):
        @pl.loop(0, 4)
        def _(cols):
            for q in range(2):
                for f4 in range(4):
                    for ri in range(2):
                        for half in range(2):
                            value = cross[f4 * 2 + ri, q, pl.ds(2 * cols + half, FINE, stride=8), :]
                            rows = pl.ds(ri * BINS + (q * 4 + f4) * FINE, FINE)
                            rhs[rows, pl.ds(half * LANES, LANES)] = value.astype(bf16)
            even = jnp.dot(table[:, :BINS], rhs[:BINS], preferred_element_type=f32)
            odd = jnp.dot(table[:, BINS:], rhs[BINS:], preferred_element_type=f32)
            right, left = (even + odd)[:FINE].T, (even - odd)[:FINE].T
            farthest = (even - odd)[FINE : FINE + 8].T[:, :1]
            near, far = (mirror(left[:, at : at + LANES]) for at in (0, LANES))
            sums = jnp.concatenate([jnp.where(lane_zero, farthest, far), jnp.where(lane_zero, far, near), right], 1)
            at = k * 4 + cols
            for n in range(8):
                kept[at, pl.ds(n * 16, 16)] = sums[n * 32 : n * 32 + 16]
                outgoing[at, pl.ds(n * 16, 16)] = sums[n * 32 + 16 : n * 32 + 32].astype(bf16)
            transfer(at).start()

    def finish(k):
        @pl.loop(0, 4)
        def _(cols):
            at = k * 4 + cols
            transfer(at).wait_recv()
            for half in range(2):
                for h in range(2):
                    for j in range(2):
                        spot16 = pl.ds(((half * 2 + h) * 2 + j) * 16, 16)
                        total = kept[at, spot16] + incoming[at, spot16].astype(f32)
                        channel = 2 * cols + half
                        for part in range(4):
                            row = k * 128 + (j * 2 + h) * 32 + part * 8 + channel
                            out_ref[pl.ds(row, 16, stride=256), :] = total[:, part * LANES : (part + 1) * LANES]

    for p in range(4):
        start_core_stage(p)
    for k in range(STEPS):
        for p in range(4):
            start_second(k, p)
    for p in range(4):
        take_second(0, p)
    start_group(0)
    for p in range(4):
        take_second(1, p)
    start_gather(0)
    start_group(1)
    start_back2(0)
    start_back1(0)
    start_gather(1)
    start_core(0)
    products(0, 0)
    start_back2(1)
    products(0, 1)
    start_back1(1)
    products(0, 2)
    start_core(1)
    products(0, 3)
    lags(0)
    for p in range(4):
        products(1, p)
    lags(1)
    finish(0)
    finish(1)

    @pl.loop(0, 8)
    def _(at):
        transfer(at).wait_send()

    for copy in first:
        copy.wait_send()
    for k in range(STEPS):
        for copy in cores[k] + second[k] + back2[k] + back1[k] + backc[k] + sum(gather[k], []) + group[k][0] + group[k][1]:
            copy.wait_send()


def per_device(spectra, src_block, quality):
    f32, bf16 = jnp.float32, jnp.bfloat16
    raw = spectra.reshape(8, 32, 2, 8, FINE)
    low, high = angle_tables()
    vmem, smem = (pl.BlockSpec(memory_space=space) for space in (pltpu.VMEM, pltpu.SMEM))
    dma = pltpu.SemaphoreType.DMA
    rows = lambda *s: pltpu.VMEM(s + (16, LANES), bf16)
    sems = []
    for shape in ((4,), (2, 4), (2, 4), (2, 2, 15), (2, 4, 15), (2, 4), (2, 4), (2, 4), (8,)):
        sems += [dma(shape), dma(shape)]
    tiles = pl.pallas_call(
        kernel,
        out_shape=jax.ShapeDtypeStruct((16 * STEPS * 32 * 4, LANES), f32),
        in_specs=[smem, vmem, smem] + [vmem] * 3,
        out_specs=vmem,
        scratch_shapes=[
            rows(4, 2, 2, 2, GROUP),
            rows(4, 2, 2, GROUP),
            rows(STEPS, 4, 2, 2, GROUP),
            rows(STEPS, 4, 2, GROUP),
            rows(STEPS, 4, 2, GROUP),
            rows(STEPS, 4, GROUP),
            rows(2, 2, STEPS, GROUP),
            rows(GROUP, 2),
            rows(GROUP, 2),
            rows(GROUP, 2),
            rows(GROUP, 2),
            rows(STEPS, 512),
            rows(32, GROUP),
            pltpu.VMEM((HALF_ROWS, 2 * BINS), bf16),
            pltpu.VMEM((8, 2, FINE * 8, LANES), f32),
            pltpu.VMEM((2 * BINS, 2 * LANES), bf16),
            pltpu.VMEM((8, LANES, LAG), f32),
            pltpu.VMEM((8, LANES, LAG), bf16),
            pltpu.VMEM((8, LANES, LAG), bf16),
        ]
        + sems,
        compiler_params=pltpu.CompilerParams(collective_id=0, has_side_effects=True, vmem_limit_bytes=66_000_000),
        name="correlate",
    )(src_block, raw, quality, jnp.asarray(low), jnp.asarray(high), jnp.asarray(swap_matrix()))
    tiles = tiles.reshape(16, STEPS, 4, 4, 8, LANES)
    return tiles.transpose(0, 1, 2, 4, 3, 5).reshape(16, STEPS, 32, LAG)


def solution(mesh):
    return jax.shard_map(
        per_device,
        mesh=mesh,
        in_specs=(P("tm", "chan", None, None), P(), P("chan")),
        out_specs=P("tm", None, "chan", None),
        check_vma=False,
    )
```

```python
import math

import jax
import jax.numpy as jnp
import numpy as np
from jax import lax
from jax.experimental import pallas as pl
from jax.experimental.pallas import tpu as pltpu
from jax.sharding import PartitionSpec as P

LAG = 512
STEPS = 2
WINDOWS = 16
BINS, LANES, FINE = 2048, 128, 256
HALF_ROWS = LAG // 2 + 16

MESH = pl.DeviceIdType.MESH
GROUP = 16


def pair_even(i):
    return i + 1 - 2 * (i % 2)


def pair_odd(i, n):
    return (i + 2 * (i % 2) - 1 + n) % n


def half_even(i):
    return ((i + 1) // 2) % 2


def half_odd(i):
    return i // 2


def coords(chan):
    return chan // 16, (chan // 4) % 4, (chan // 2) % 2, chan % 2


def chan_of(z, x, y, core):
    return ((z * 4 + x) * 2 + y) * 2 + core


def angle_tables():
    scale = 1.0 / math.sqrt(2.0 * BINS * WINDOWS)
    bins = np.arange(BINS, dtype=np.int64)[None, :]
    low = np.arange(8, dtype=np.int64)[:, None] * bins % (2 * BINS) * (math.pi / BINS)
    high = np.arange(0, HALF_ROWS, 8, dtype=np.int64)[:, None] * bins % (2 * BINS) * (math.pi / BINS)
    f32 = np.float32
    return (np.stack([np.cos(low), np.sin(low)]) * scale).astype(f32), np.stack([np.cos(high), np.sin(high)]).astype(f32)


def swap_matrix():
    lane = np.arange(LANES)
    swap = np.zeros((LANES, LANES), np.float32)
    imag = lane // 8 % 2
    swap[lane ^ 8, lane] = np.where(imag == 0, 1.0, -1.0)
    return swap.astype(jnp.bfloat16)


def kernel(
    blk_ref, raw_ref, quality_ref, low_ref, high_ref, swap_ref, out_ref,
    own, r1, cur1, rc, cur2, r2, cur3, rm00, rm01, rm10, rm11, src,
    swapped, table, cross, rhs, kept, outgoing, incoming, *sems,
):
    s1s, s1r, scs, scr, s2s, s2r, sms, smr, gms, gmr, g2s, g2r, g1s, g1r, gcs, gcr, xs, xr = sems
    f32, bf16 = jnp.float32, jnp.bfloat16
    tm = lax.axis_index("tm")
    z, x, y, core = coords(lax.axis_index("chan"))
    z_even, z_odd = pair_even(z), pair_odd(z, 8)
    x_even, x_odd = pair_even(x), pair_odd(x, 4)
    z_half = z % 2
    at_xe, at_xo = chan_of(z, x_even, y, core), chan_of(z, x_odd, y, core)
    at_ze, at_zo = chan_of(z_even, x, y, core), chan_of(z_odd, x, y, core)
    at_core = chan_of(z, x, y, 1 - core)
    parts = [
        (at_xe, at_ze, half_even(x), z_half),
        (at_ze, at_xe, z_half, half_even(x)),
        (at_xo, at_zo, half_odd(x), z_half),
        (at_zo, at_xo, z_half, half_odd(x)),
    ]
    mine = [half_odd(x) * 8 + y * 4 + z // 2, half_even(x) * 8 + y * 4 + z // 2]
    peers = [[], []]
    for pair in range(2):
        for offset in range(1, GROUP):
            d_x, d_y, d_z = offset // 8, (offset // 4) % 2, offset % 4
            far_x = (x_odd, x_even)[pair] if d_x else x
            peer_z = z_half + 2 * ((z // 2 + d_z) % 4)
            peer_y = (y + d_y) % 2
            half = (half_odd(far_x), half_even(far_x))[pair]
            peers[pair].append((chan_of(peer_z, far_x, peer_y, core), half * 8 + peer_y * 4 + peer_z // 2))

    barrier = pltpu.get_barrier_semaphore()
    greet = [at_ze, at_zo, at_core] + [c for c, _ in peers[0]] + [c for c, _ in peers[1][7:]]
    for to in greet:
        pl.semaphore_signal(barrier, inc=1, device_id={"chan": to}, device_id_type=MESH)
    pl.semaphore_signal(barrier, inc=1, device_id={"tm": 1 - tm}, device_id_type=MESH)

    @pl.loop(0, 8)
    def _(i):
        for u in range(4):
            c = 4 * i + u
            value = raw_ref[:, c].astype(f32).reshape(LANES, FINE).T * quality_ref[c].astype(f32)
            for p in range(4):
                cross[p // 2, p % 2, pl.ds(c, 64, stride=32), :] = value[64 * p : 64 * p + 64]

    def add_power(i, total):
        for p in range(4):
            for u in range(4):
                v = cross[p // 2, p % 2, pl.ds(pl.multiple_of(i * 128 + u * 32, 32), 32), :]
                total = total + v * v
        return total

    power = lax.fori_loop(0, 16, add_power, jnp.zeros((32, LANES), f32))
    lane1 = lax.broadcasted_iota(jnp.int32, (32, LANES), 1)
    for shift in (1, 2, 4, 8):
        other = jnp.where(lane1 // shift % 2 == 0, pltpu.roll(power, LANES - shift, 1), pltpu.roll(power, shift, 1))
        power = power + other
    scale = 1.0 / jnp.sqrt(power / (2.0 * BINS) + 1e-06)
    for p in range(4):

        @pl.loop(0, 8)
        def _(i):
            for u in range(8):
                v = cross[p // 2, p % 2, pl.ds(pl.multiple_of(i * 256 + u * 32, 32), 32), :] * scale
                for j in range(2):
                    own[p, i // 4, i // 2 % 2, i % 2, 2 * u + j] = v[16 * j : 16 * j + 16].astype(bf16)

    pl.semaphore_wait(barrier, len(greet) + 1)

    roots = [coords(blk_ref[k]) for k in range(STEPS)]
    from_xe = [r[1] == x_even for r in roots]
    from_xo = [r[1] == x_odd for r in roots]
    from_ze = [r[0] == z_even for r in roots]
    from_zo = [r[0] == z_odd for r in roots]
    from_core = [r[3] != core for r in roots]
    first_from = [from_xe, from_ze, from_xo, from_zo]
    second_from = [from_ze, from_xe, from_zo, from_xo]
    chosen = []
    for pair in range(2):
        row = []
        for r in roots:
            if pair == 0:
                row.append(half_odd(r[1]) * 8 + r[2] * 4 + r[0] // 2)
            else:
                z_in = jnp.where(r[0] % 2 == z_half, r[0] // 2, pair_odd(r[0], 8) // 2)
                row.append(half_even(r[1]) * 8 + r[2] * 4 + z_in)
        chosen.append(row)
    rm = ((rm00, rm01), (rm10, rm11))

    def send(src_ref, dst_ref, ssem, rsem, to):
        copy = pltpu.make_async_remote_copy(
            src_ref=src_ref, dst_ref=dst_ref, send_sem=ssem, recv_sem=rsem,
            device_id={"chan": to}, device_id_type=MESH,
        )
        copy.start()
        return copy

    first = []
    for p, (to, _, b1, _) in enumerate(parts):
        first.append(send(own.at[p, :, 1 - b1], r1.at[p], s1s.at[p], s1r.at[p], to))

    @pl.loop(0, HALF_ROWS // 16)
    def _(i):
        for part in range(BINS // 512):
            lanes = pl.ds(part * 512, 512)
            lc, ls = low_ref[0, :, lanes], low_ref[1, :, lanes]
            cos, sin = [], []
            for h in range(2):
                hc, hs = high_ref[0, pl.ds(2 * i + h, 1), lanes], high_ref[1, pl.ds(2 * i + h, 1), lanes]
                cos.append(lc * hc - ls * hs)
                sin.append(-(ls * hc + lc * hs))
            rows = pl.ds(pl.multiple_of(i * 16, 16), 16)
            table[rows, lanes] = jnp.concatenate(cos, 0).astype(bf16)
            table[rows, pl.ds(BINS + part * 512, 512)] = jnp.concatenate(sin, 0).astype(bf16)

    for p in range(4):

        @pl.loop(0, 8)
        def _(i):
            chunk = own[p, i // 4, i // 2 % 2, i % 2].reshape(256, LANES)
            swapped[8 * p + i] = (
                jnp.dot(chunk, swap_ref[...], preferred_element_type=f32).astype(bf16).reshape(GROUP, 16, LANES)
            )

    cores, second, group, gather, back2, back1, backc = ([[None] * 4 for _ in range(STEPS)] for _ in range(7))

    def start_core_stage(p):
        _, _, b1, _ = parts[p]
        first[p].wait_recv()

        @pl.loop(0, GROUP)
        def _(m):
            held, got = own[p, :, b1, :, m], r1[p, :, :, m]
            for k in range(STEPS):
                cur1[k, p, :, :, m] = jnp.where(first_from[p][k], got, held)

        for k in range(STEPS):
            cores[k][p] = send(cur1.at[k, p, 1 - core], rc.at[k, p], scs.at[k, p], scr.at[k, p], at_core)

    def start_second(k, p):
        _, to, _, b2 = parts[p]
        cores[k][p].wait_recv()

        @pl.loop(0, GROUP)
        def _(m):
            cur2[k, p, :, m] = jnp.where(from_core[k], rc[k, p, :, m], cur1[k, p, core, :, m])

        second[k][p] = send(cur2.at[k, p, 1 - b2], r2.at[k, p], s2s.at[k, p], s2r.at[k, p], to)

    def take_second(k, p):
        b2 = parts[p][3]
        second[k][p].wait_recv()

        @pl.loop(0, GROUP)
        def _(m):
            cur3[p // 2, p % 2, k, m] = jnp.where(second_from[p][k], r2[k, p, m], cur2[k, p, b2, m])

    def start_group(k):
        for pair in range(2):
            at = mine[pair]
            group[k][pair] = [
                send(cur3.at[pair, :, k, slot], rm[pair][k].at[at], sms.at[k, pair, j], smr.at[k, pair, j], to)
                for j, (to, slot) in enumerate(peers[pair])
            ]
            rm[pair][k][at] = cur3[pair, :, k, at]

    def spot(k, p, level):
        _, _, b1, b2 = parts[p]
        if level == 0:
            return src.at[k, pl.ds((((p * 2 + core) * 2 + b1) * 2 + b2) * 16 + mine[p // 2], 1)]
        if level == 1:
            return src.at[k, pl.ds((((p * 2 + core) * 2 + b1) * 2 + b2) * 16, 16)]
        if level == 2:
            return src.at[k, pl.ds(((p * 2 + core) * 2 + b1) * 32, 32)]
        return src.at[k, pl.ds((p * 2 + core) * 64, 64)]

    def start_gather(k):
        for pair in range(2):
            for copy in group[k][pair]:
                copy.wait_recv()
            for p in (2 * pair, 2 * pair + 1):
                _, _, b1, b2 = parts[p]
                at = (((p * 2 + core) * 2 + b1) * 2 + b2) * 16 + mine[pair]
                src[k, at] = rm[pair][k][chosen[pair][k], p % 2]
                gather[k][p] = [
                    send(spot(k, p, 0), spot(k, p, 0), gms.at[k, p, j], gmr.at[k, p, j], to)
                    for j, (to, _) in enumerate(peers[pair])
                ]

    def start_back2(k):
        for p in range(4):
            for copy in gather[k][p]:
                copy.wait_recv()
            back2[k][p] = send(spot(k, p, 1), spot(k, p, 1), g2s.at[k, p], g2r.at[k, p], parts[p][1])

    def start_back1(k):
        for p in range(4):
            back2[k][p].wait_recv()
            back1[k][p] = send(spot(k, p, 2), spot(k, p, 2), g1s.at[k, p], g1r.at[k, p], parts[p][0])

    def start_core(k):
        for p in range(4):
            back1[k][p].wait_recv()
            backc[k][p] = send(spot(k, p, 3), spot(k, p, 3), gcs.at[k, p], gcr.at[k, p], at_core)

    lane2 = lax.broadcasted_iota(jnp.int32, (1, 2 * LANES), 1)
    lane0 = lax.broadcasted_iota(jnp.int32, (1, LANES), 1)
    fmask = [(lane2 % 4 == f4).astype(f32).astype(bf16) for f4 in range(4)]
    qmask = [(lane0 // 4 % 2 == q).astype(f32).astype(bf16) for q in range(2)]
    zero = jnp.zeros((32, LANES), bf16)
    low_lane = lax.broadcasted_iota(jnp.int32, (8, LANES), 1) < 64

    def products(k, p):
        backc[k][p].wait_recv()

        @pl.loop(0, 4)
        def _(half_i):
            for uu in range(16):
                i, u = half_i * 2 + uu // 8, uu % 8
                real = [own[p, half_i // 2, half_i % 2, uu // 8, 2 * u + j] for j in range(2)]
                imag = [swapped[8 * p + i, 2 * u + j] for j in range(2)]
                pieces = [jnp.concatenate(v, 1) for v in (real, imag)]
                lhs = jnp.concatenate([v * fmask[f4] for f4 in range(4) for v in pieces], 0)
                at = p * 128 + i * 16 + 2 * u
                sources = jnp.concatenate([src[k, at + h] for h in (tm, 1 - tm)], 0)
                rows = []
                for q in range(2):
                    masked = sources * qmask[q]
                    rows += [jnp.concatenate([masked, zero], 1), jnp.concatenate([zero, masked], 1)]
                weights = jnp.concatenate(rows, 0)
                product = lax.dot_general(lhs, weights, (((1,), (1,)), ((), ())), preferred_element_type=f32)
                row = pl.multiple_of((p * 64 + i * 8 + u) * 8, 8)
                for n in range(8):
                    upper, lower = product[16 * n : 16 * n + 8], product[16 * n + 8 : 16 * n + 16]
                    cross[n, 0, pl.ds(row, 8), :] = jnp.where(low_lane, upper, pltpu.roll(lower, 64, 1))
                    cross[n, 1, pl.ds(row, 8), :] = jnp.where(low_lane, pltpu.roll(upper, 64, 1), lower)

    def transfer(at):
        return pltpu.make_async_remote_copy(
            src_ref=outgoing.at[at], dst_ref=incoming.at[at], send_sem=xs.at[at], recv_sem=xr.at[at],
            device_id={"tm": 1 - tm}, device_id_type=MESH,
        )

    lane3 = lax.broadcasted_iota(jnp.int32, (FINE, LANES), 1)
    lane_zero, mirrored = lane3 == 0, (LANES - lane3) % LANES

    def mirror(value):
        return jnp.take_along_axis(value, mirrored, axis=1, mode="promise_in_bounds")

    def lags(k):
        @pl.loop(0, 4)
        def _(cols):
            for q in range(2):
                for f4 in range(4):
                    for ri in range(2):
                        for half in range(2):
                            value = cross[f4 * 2 + ri, q, pl.ds(2 * cols + half, FINE, stride=8), :]
                            rows = pl.ds(ri * BINS + (q * 4 + f4) * FINE, FINE)
                            rhs[rows, pl.ds(half * LANES, LANES)] = value.astype(bf16)
            even = jnp.dot(table[:, :BINS], rhs[:BINS], preferred_element_type=f32)
            odd = jnp.dot(table[:, BINS:], rhs[BINS:], preferred_element_type=f32)
            right, left = (even + odd)[:FINE].T, (even - odd)[:FINE].T
            farthest = (even - odd)[FINE : FINE + 8].T[:, :1]
            near, far = (mirror(left[:, at : at + LANES]) for at in (0, LANES))
            sums = jnp.concatenate([jnp.where(lane_zero, farthest, far), jnp.where(lane_zero, far, near), right], 1)
            at = k * 4 + cols
            for n in range(8):
                kept[at, pl.ds(n * 16, 16)] = sums[n * 32 : n * 32 + 16]
                outgoing[at, pl.ds(n * 16, 16)] = sums[n * 32 + 16 : n * 32 + 32].astype(bf16)
            transfer(at).start()

    def finish(k):
        @pl.loop(0, 4)
        def _(cols):
            at = k * 4 + cols
            transfer(at).wait_recv()
            for half in range(2):
                for h in range(2):
                    for j in range(2):
                        spot16 = pl.ds(((half * 2 + h) * 2 + j) * 16, 16)
                        total = kept[at, spot16] + incoming[at, spot16].astype(f32)
                        channel = 2 * cols + half
                        for part in range(4):
                            row = k * 128 + (j * 2 + h) * 32 + part * 8 + channel
                            out_ref[pl.ds(row, 16, stride=256), :] = total[:, part * LANES : (part + 1) * LANES]

    for p in range(4):
        start_core_stage(p)
    for k in range(STEPS):
        for p in range(4):
            start_second(k, p)
    for p in range(4):
        take_second(0, p)
    start_group(0)
    for p in range(4):
        take_second(1, p)
    start_gather(0)
    start_group(1)
    start_back2(0)
    start_back1(0)
    start_gather(1)
    start_core(0)
    products(0, 0)
    start_back2(1)
    products(0, 1)
    start_back1(1)
    products(0, 2)
    start_core(1)
    products(0, 3)
    lags(0)
    for p in range(4):
        products(1, p)
    lags(1)
    finish(0)
    finish(1)

    @pl.loop(0, 8)
    def _(at):
        transfer(at).wait_send()

    for copy in first:
        copy.wait_send()
    for k in range(STEPS):
        for copy in cores[k] + second[k] + back2[k] + back1[k] + backc[k] + sum(gather[k], []) + group[k][0] + group[k][1]:
            copy.wait_send()


def per_device(spectra, src_block, quality):
    f32, bf16 = jnp.float32, jnp.bfloat16
    raw = spectra
    low, high = angle_tables()
    vmem, smem = (pl.BlockSpec(memory_space=space) for space in (pltpu.VMEM, pltpu.SMEM))
    dma = pltpu.SemaphoreType.DMA
    rows = lambda *s: pltpu.VMEM(s + (16, LANES), bf16)
    sems = []
    for shape in ((4,), (2, 4), (2, 4), (2, 2, 15), (2, 4, 15), (2, 4), (2, 4), (2, 4), (8,)):
        sems += [dma(shape), dma(shape)]
    tiles = pl.pallas_call(
        kernel,
        out_shape=jax.ShapeDtypeStruct((16 * STEPS * 32 * 4, LANES), f32),
        in_specs=[smem, vmem, smem] + [vmem] * 3,
        out_specs=vmem,
        scratch_shapes=[
            rows(4, 2, 2, 2, GROUP),
            rows(4, 2, 2, GROUP),
            rows(STEPS, 4, 2, 2, GROUP),
            rows(STEPS, 4, 2, GROUP),
            rows(STEPS, 4, 2, GROUP),
            rows(STEPS, 4, GROUP),
            rows(2, 2, STEPS, GROUP),
            rows(GROUP, 2),
            rows(GROUP, 2),
            rows(GROUP, 2),
            rows(GROUP, 2),
            rows(STEPS, 512),
            rows(32, GROUP),
            pltpu.VMEM((HALF_ROWS, 2 * BINS), bf16),
            pltpu.VMEM((8, 2, FINE * 8, LANES), f32),
            pltpu.VMEM((2 * BINS, 2 * LANES), bf16),
            pltpu.VMEM((8, LANES, LAG), f32),
            pltpu.VMEM((8, LANES, LAG), bf16),
            pltpu.VMEM((8, LANES, LAG), bf16),
        ]
        + sems,
        compiler_params=pltpu.CompilerParams(collective_id=0, has_side_effects=True, vmem_limit_bytes=66_000_000),
        name="correlate",
    )(src_block, raw, quality, jnp.asarray(low), jnp.asarray(high), jnp.asarray(swap_matrix()))
    tiles = tiles.reshape(16, STEPS, 4, 4, 8, LANES)
    return tiles.transpose(0, 1, 2, 4, 3, 5).reshape(16, STEPS, 32, LAG)


def solution(mesh):
    return jax.shard_map(
        per_device,
        mesh=mesh,
        in_specs=(P("tm", "chan", None, None), P(), P("chan")),
        out_specs=P("tm", None, "chan", None),
        check_vma=False,
    )
```

```python
import math

import jax
import jax.numpy as jnp
import numpy as np
from jax import lax
from jax.experimental import pallas as pl
from jax.experimental.pallas import tpu as pltpu
from jax.sharding import PartitionSpec as P

LAG = 512
STEPS = 2
WINDOWS = 16
BINS, LANES, FINE = 2048, 128, 256
HALF_ROWS = LAG // 2 + 16

MESH = pl.DeviceIdType.MESH
GROUP = 16


def pair_even(i):
    return i + 1 - 2 * (i % 2)


def pair_odd(i, n):
    return (i + 2 * (i % 2) - 1 + n) % n


def half_even(i):
    return ((i + 1) // 2) % 2


def half_odd(i):
    return i // 2


def coords(chan):
    return chan // 16, (chan // 4) % 4, (chan // 2) % 2, chan % 2


def chan_of(z, x, y, core):
    return ((z * 4 + x) * 2 + y) * 2 + core


def angle_tables():
    scale = 1.0 / math.sqrt(2.0 * BINS * WINDOWS)
    bins = np.arange(BINS, dtype=np.int64)[None, :]
    low = np.arange(8, dtype=np.int64)[:, None] * bins % (2 * BINS) * (math.pi / BINS)
    high = np.arange(0, HALF_ROWS, 8, dtype=np.int64)[:, None] * bins % (2 * BINS) * (math.pi / BINS)
    f32 = np.float32
    return (np.stack([np.cos(low), np.sin(low)]) * scale).astype(f32), np.stack([np.cos(high), np.sin(high)]).astype(f32)


def swap_matrix():
    lane = np.arange(LANES)
    swap = np.zeros((LANES, LANES), np.float32)
    imag = lane // 8 % 2
    swap[lane ^ 8, lane] = np.where(imag == 0, 1.0, -1.0)
    return swap.astype(jnp.bfloat16)


def kernel(
    blk_ref, spectra_ref, quality_ref, low_ref, high_ref, swap_ref, out_ref,
    raw_ref, load_sem, own, r1, cur1, rc, cur2, r2, cur3, rm00, rm01, rm10, rm11, src,
    swapped, table, cross, rhs, kept, outgoing, incoming, *sems,
):
    s1s, s1r, scs, scr, s2s, s2r, sms, smr, gms, gmr, g2s, g2r, g1s, g1r, gcs, gcr, xs, xr = sems
    f32, bf16 = jnp.float32, jnp.bfloat16
    def load(i):
        channels = pl.ds(4 * i, 4)
        return pltpu.make_async_copy(spectra_ref.at[:, channels], raw_ref.at[:, channels], load_sem.at[i])

    for i in range(8):
        load(i).start()
    tm = lax.axis_index("tm")
    z, x, y, core = coords(lax.axis_index("chan"))
    z_even, z_odd = pair_even(z), pair_odd(z, 8)
    x_even, x_odd = pair_even(x), pair_odd(x, 4)
    z_half = z % 2
    at_xe, at_xo = chan_of(z, x_even, y, core), chan_of(z, x_odd, y, core)
    at_ze, at_zo = chan_of(z_even, x, y, core), chan_of(z_odd, x, y, core)
    at_core = chan_of(z, x, y, 1 - core)
    parts = [
        (at_xe, at_ze, half_even(x), z_half),
        (at_ze, at_xe, z_half, half_even(x)),
        (at_xo, at_zo, half_odd(x), z_half),
        (at_zo, at_xo, z_half, half_odd(x)),
    ]
    mine = [half_odd(x) * 8 + y * 4 + z // 2, half_even(x) * 8 + y * 4 + z // 2]
    peers = [[], []]
    for pair in range(2):
        for offset in range(1, GROUP):
            d_x, d_y, d_z = offset // 8, (offset // 4) % 2, offset % 4
            far_x = (x_odd, x_even)[pair] if d_x else x
            peer_z = z_half + 2 * ((z // 2 + d_z) % 4)
            peer_y = (y + d_y) % 2
            half = (half_odd(far_x), half_even(far_x))[pair]
            peers[pair].append((chan_of(peer_z, far_x, peer_y, core), half * 8 + peer_y * 4 + peer_z // 2))

    barrier = pltpu.get_barrier_semaphore()
    greet = [at_ze, at_zo, at_core] + [c for c, _ in peers[0]] + [c for c, _ in peers[1][7:]]
    for to in greet:
        pl.semaphore_signal(barrier, inc=1, device_id={"chan": to}, device_id_type=MESH)
    pl.semaphore_signal(barrier, inc=1, device_id={"tm": 1 - tm}, device_id_type=MESH)

    @pl.loop(0, 8)
    def _(i):
        load(i).wait()
        for u in range(4):
            c = 4 * i + u
            value = raw_ref[:, c].astype(f32).reshape(LANES, FINE).T * quality_ref[c].astype(f32)
            for p in range(4):
                cross[p // 2, p % 2, pl.ds(c, 64, stride=32), :] = value[64 * p : 64 * p + 64]

    def add_power(i, total):
        for p in range(4):
            for u in range(4):
                v = cross[p // 2, p % 2, pl.ds(pl.multiple_of(i * 128 + u * 32, 32), 32), :]
                total = total + v * v
        return total

    power = lax.fori_loop(0, 16, add_power, jnp.zeros((32, LANES), f32))
    lane1 = lax.broadcasted_iota(jnp.int32, (32, LANES), 1)
    for shift in (1, 2, 4, 8):
        other = jnp.where(lane1 // shift % 2 == 0, pltpu.roll(power, LANES - shift, 1), pltpu.roll(power, shift, 1))
        power = power + other
    scale = 1.0 / jnp.sqrt(power / (2.0 * BINS) + 1e-06)
    for p in range(4):

        @pl.loop(0, 8)
        def _(i):
            for u in range(8):
                v = cross[p // 2, p % 2, pl.ds(pl.multiple_of(i * 256 + u * 32, 32), 32), :] * scale
                for j in range(2):
                    own[p, i // 4, i // 2 % 2, i % 2, 2 * u + j] = v[16 * j : 16 * j + 16].astype(bf16)

    pl.semaphore_wait(barrier, len(greet) + 1)

    roots = [coords(blk_ref[k]) for k in range(STEPS)]
    from_xe = [r[1] == x_even for r in roots]
    from_xo = [r[1] == x_odd for r in roots]
    from_ze = [r[0] == z_even for r in roots]
    from_zo = [r[0] == z_odd for r in roots]
    from_core = [r[3] != core for r in roots]
    first_from = [from_xe, from_ze, from_xo, from_zo]
    second_from = [from_ze, from_xe, from_zo, from_xo]
    chosen = []
    for pair in range(2):
        row = []
        for r in roots:
            if pair == 0:
                row.append(half_odd(r[1]) * 8 + r[2] * 4 + r[0] // 2)
            else:
                z_in = jnp.where(r[0] % 2 == z_half, r[0] // 2, pair_odd(r[0], 8) // 2)
                row.append(half_even(r[1]) * 8 + r[2] * 4 + z_in)
        chosen.append(row)
    rm = ((rm00, rm01), (rm10, rm11))

    def send(src_ref, dst_ref, ssem, rsem, to):
        copy = pltpu.make_async_remote_copy(
            src_ref=src_ref, dst_ref=dst_ref, send_sem=ssem, recv_sem=rsem,
            device_id={"chan": to}, device_id_type=MESH,
        )
        copy.start()
        return copy

    first = []
    for p, (to, _, b1, _) in enumerate(parts):
        first.append(send(own.at[p, :, 1 - b1], r1.at[p], s1s.at[p], s1r.at[p], to))

    @pl.loop(0, HALF_ROWS // 16)
    def _(i):
        for part in range(BINS // 512):
            lanes = pl.ds(part * 512, 512)
            lc, ls = low_ref[0, :, lanes], low_ref[1, :, lanes]
            cos, sin = [], []
            for h in range(2):
                hc, hs = high_ref[0, pl.ds(2 * i + h, 1), lanes], high_ref[1, pl.ds(2 * i + h, 1), lanes]
                cos.append(lc * hc - ls * hs)
                sin.append(-(ls * hc + lc * hs))
            rows = pl.ds(pl.multiple_of(i * 16, 16), 16)
            table[rows, lanes] = jnp.concatenate(cos, 0).astype(bf16)
            table[rows, pl.ds(BINS + part * 512, 512)] = jnp.concatenate(sin, 0).astype(bf16)

    for p in range(4):

        @pl.loop(0, 8)
        def _(i):
            chunk = own[p, i // 4, i // 2 % 2, i % 2].reshape(256, LANES)
            swapped[8 * p + i] = (
                jnp.dot(chunk, swap_ref[...], preferred_element_type=f32).astype(bf16).reshape(GROUP, 16, LANES)
            )

    cores, second, group, gather, back2, back1, backc = ([[None] * 4 for _ in range(STEPS)] for _ in range(7))

    def start_core_stage(p):
        _, _, b1, _ = parts[p]
        first[p].wait_recv()

        @pl.loop(0, GROUP)
        def _(m):
            held, got = own[p, :, b1, :, m], r1[p, :, :, m]
            for k in range(STEPS):
                cur1[k, p, :, :, m] = jnp.where(first_from[p][k], got, held)

        for k in range(STEPS):
            cores[k][p] = send(cur1.at[k, p, 1 - core], rc.at[k, p], scs.at[k, p], scr.at[k, p], at_core)

    def start_second(k, p):
        _, to, _, b2 = parts[p]
        cores[k][p].wait_recv()

        @pl.loop(0, GROUP)
        def _(m):
            cur2[k, p, :, m] = jnp.where(from_core[k], rc[k, p, :, m], cur1[k, p, core, :, m])

        second[k][p] = send(cur2.at[k, p, 1 - b2], r2.at[k, p], s2s.at[k, p], s2r.at[k, p], to)

    def take_second(k, p):
        b2 = parts[p][3]
        second[k][p].wait_recv()

        @pl.loop(0, GROUP)
        def _(m):
            cur3[p // 2, p % 2, k, m] = jnp.where(second_from[p][k], r2[k, p, m], cur2[k, p, b2, m])

    def start_group(k):
        for pair in range(2):
            at = mine[pair]
            group[k][pair] = [
                send(cur3.at[pair, :, k, slot], rm[pair][k].at[at], sms.at[k, pair, j], smr.at[k, pair, j], to)
                for j, (to, slot) in enumerate(peers[pair])
            ]
            rm[pair][k][at] = cur3[pair, :, k, at]

    def spot(k, p, level):
        _, _, b1, b2 = parts[p]
        if level == 0:
            return src.at[k, pl.ds((((p * 2 + core) * 2 + b1) * 2 + b2) * 16 + mine[p // 2], 1)]
        if level == 1:
            return src.at[k, pl.ds((((p * 2 + core) * 2 + b1) * 2 + b2) * 16, 16)]
        if level == 2:
            return src.at[k, pl.ds(((p * 2 + core) * 2 + b1) * 32, 32)]
        return src.at[k, pl.ds((p * 2 + core) * 64, 64)]

    def start_gather(k):
        for pair in range(2):
            for copy in group[k][pair]:
                copy.wait_recv()
            for p in (2 * pair, 2 * pair + 1):
                _, _, b1, b2 = parts[p]
                at = (((p * 2 + core) * 2 + b1) * 2 + b2) * 16 + mine[pair]
                src[k, at] = rm[pair][k][chosen[pair][k], p % 2]
                gather[k][p] = [
                    send(spot(k, p, 0), spot(k, p, 0), gms.at[k, p, j], gmr.at[k, p, j], to)
                    for j, (to, _) in enumerate(peers[pair])
                ]

    def start_back2(k):
        for p in range(4):
            for copy in gather[k][p]:
                copy.wait_recv()
            back2[k][p] = send(spot(k, p, 1), spot(k, p, 1), g2s.at[k, p], g2r.at[k, p], parts[p][1])

    def start_back1(k):
        for p in range(4):
            back2[k][p].wait_recv()
            back1[k][p] = send(spot(k, p, 2), spot(k, p, 2), g1s.at[k, p], g1r.at[k, p], parts[p][0])

    def start_core(k):
        for p in range(4):
            back1[k][p].wait_recv()
            backc[k][p] = send(spot(k, p, 3), spot(k, p, 3), gcs.at[k, p], gcr.at[k, p], at_core)

    lane2 = lax.broadcasted_iota(jnp.int32, (1, 2 * LANES), 1)
    lane0 = lax.broadcasted_iota(jnp.int32, (1, LANES), 1)
    fmask = [(lane2 % 4 == f4).astype(f32).astype(bf16) for f4 in range(4)]
    qmask = [(lane0 // 4 % 2 == q).astype(f32).astype(bf16) for q in range(2)]
    zero = jnp.zeros((32, LANES), bf16)
    low_lane = lax.broadcasted_iota(jnp.int32, (8, LANES), 1) < 64

    def products(k, p):
        backc[k][p].wait_recv()

        @pl.loop(0, 4)
        def _(half_i):
            for uu in range(16):
                i, u = half_i * 2 + uu // 8, uu % 8
                real = [own[p, half_i // 2, half_i % 2, uu // 8, 2 * u + j] for j in range(2)]
                imag = [swapped[8 * p + i, 2 * u + j] for j in range(2)]
                pieces = [jnp.concatenate(v, 1) for v in (real, imag)]
                lhs = jnp.concatenate([v * fmask[f4] for f4 in range(4) for v in pieces], 0)
                at = p * 128 + i * 16 + 2 * u
                sources = jnp.concatenate([src[k, at + h] for h in (tm, 1 - tm)], 0)
                rows = []
                for q in range(2):
                    masked = sources * qmask[q]
                    rows += [jnp.concatenate([masked, zero], 1), jnp.concatenate([zero, masked], 1)]
                weights = jnp.concatenate(rows, 0)
                product = lax.dot_general(lhs, weights, (((1,), (1,)), ((), ())), preferred_element_type=f32)
                row = pl.multiple_of((p * 64 + i * 8 + u) * 8, 8)
                for n in range(8):
                    upper, lower = product[16 * n : 16 * n + 8], product[16 * n + 8 : 16 * n + 16]
                    cross[n, 0, pl.ds(row, 8), :] = jnp.where(low_lane, upper, pltpu.roll(lower, 64, 1))
                    cross[n, 1, pl.ds(row, 8), :] = jnp.where(low_lane, pltpu.roll(upper, 64, 1), lower)

    def transfer(at):
        return pltpu.make_async_remote_copy(
            src_ref=outgoing.at[at], dst_ref=incoming.at[at], send_sem=xs.at[at], recv_sem=xr.at[at],
            device_id={"tm": 1 - tm}, device_id_type=MESH,
        )

    lane3 = lax.broadcasted_iota(jnp.int32, (FINE, LANES), 1)
    lane_zero, mirrored = lane3 == 0, (LANES - lane3) % LANES

    def mirror(value):
        return jnp.take_along_axis(value, mirrored, axis=1, mode="promise_in_bounds")

    def lags(k):
        @pl.loop(0, 4)
        def _(cols):
            for q in range(2):
                for f4 in range(4):
                    for ri in range(2):
                        for half in range(2):
                            value = cross[f4 * 2 + ri, q, pl.ds(2 * cols + half, FINE, stride=8), :]
                            rows = pl.ds(ri * BINS + (q * 4 + f4) * FINE, FINE)
                            rhs[rows, pl.ds(half * LANES, LANES)] = value.astype(bf16)
            even = jnp.dot(table[:, :BINS], rhs[:BINS], preferred_element_type=f32)
            odd = jnp.dot(table[:, BINS:], rhs[BINS:], preferred_element_type=f32)
            right, left = (even + odd)[:FINE].T, (even - odd)[:FINE].T
            farthest = (even - odd)[FINE : FINE + 8].T[:, :1]
            near, far = (mirror(left[:, at : at + LANES]) for at in (0, LANES))
            sums = jnp.concatenate([jnp.where(lane_zero, farthest, far), jnp.where(lane_zero, far, near), right], 1)
            at = k * 4 + cols
            for n in range(8):
                kept[at, pl.ds(n * 16, 16)] = sums[n * 32 : n * 32 + 16]
                outgoing[at, pl.ds(n * 16, 16)] = sums[n * 32 + 16 : n * 32 + 32].astype(bf16)
            transfer(at).start()

    def finish(k):
        @pl.loop(0, 4)
        def _(cols):
            at = k * 4 + cols
            transfer(at).wait_recv()
            for half in range(2):
                for h in range(2):
                    for j in range(2):
                        spot16 = pl.ds(((half * 2 + h) * 2 + j) * 16, 16)
                        total = kept[at, spot16] + incoming[at, spot16].astype(f32)
                        channel = 2 * cols + half
                        for part in range(4):
                            row = k * 128 + (j * 2 + h) * 32 + part * 8 + channel
                            out_ref[pl.ds(row, 16, stride=256), :] = total[:, part * LANES : (part + 1) * LANES]

    for p in range(4):
        start_core_stage(p)
    for k in range(STEPS):
        for p in range(4):
            start_second(k, p)
    for p in range(4):
        take_second(0, p)
    start_group(0)
    for p in range(4):
        take_second(1, p)
    start_gather(0)
    start_group(1)
    start_back2(0)
    start_back1(0)
    start_gather(1)
    start_core(0)
    products(0, 0)
    start_back2(1)
    products(0, 1)
    start_back1(1)
    products(0, 2)
    start_core(1)
    products(0, 3)
    lags(0)
    for p in range(4):
        products(1, p)
    lags(1)
    finish(0)
    finish(1)

    @pl.loop(0, 8)
    def _(at):
        transfer(at).wait_send()

    for copy in first:
        copy.wait_send()
    for k in range(STEPS):
        for copy in cores[k] + second[k] + back2[k] + back1[k] + backc[k] + sum(gather[k], []) + group[k][0] + group[k][1]:
            copy.wait_send()


def per_device(spectra, src_block, quality):
    f32, bf16 = jnp.float32, jnp.bfloat16
    raw = spectra
    low, high = angle_tables()
    vmem, smem = (pl.BlockSpec(memory_space=space) for space in (pltpu.VMEM, pltpu.SMEM))
    dma = pltpu.SemaphoreType.DMA
    rows = lambda *s: pltpu.VMEM(s + (16, LANES), bf16)
    sems = []
    for shape in ((4,), (2, 4), (2, 4), (2, 2, 15), (2, 4, 15), (2, 4), (2, 4), (2, 4), (8,)):
        sems += [dma(shape), dma(shape)]
    tiles = pl.pallas_call(
        kernel,
        out_shape=jax.ShapeDtypeStruct((16 * STEPS * 32 * 4, LANES), f32),
        in_specs=[smem, pl.BlockSpec(memory_space=pl.ANY), smem] + [vmem] * 3,
        out_specs=vmem,
        scratch_shapes=[
            pltpu.VMEM(spectra.shape, bf16),
            dma((8,)),
            rows(4, 2, 2, 2, GROUP),
            rows(4, 2, 2, GROUP),
            rows(STEPS, 4, 2, 2, GROUP),
            rows(STEPS, 4, 2, GROUP),
            rows(STEPS, 4, 2, GROUP),
            rows(STEPS, 4, GROUP),
            rows(2, 2, STEPS, GROUP),
            rows(GROUP, 2),
            rows(GROUP, 2),
            rows(GROUP, 2),
            rows(GROUP, 2),
            rows(STEPS, 512),
            rows(32, GROUP),
            pltpu.VMEM((HALF_ROWS, 2 * BINS), bf16),
            pltpu.VMEM((8, 2, FINE * 8, LANES), f32),
            pltpu.VMEM((2 * BINS, 2 * LANES), bf16),
            pltpu.VMEM((8, LANES, LAG), f32),
            pltpu.VMEM((8, LANES, LAG), bf16),
            pltpu.VMEM((8, LANES, LAG), bf16),
        ]
        + sems,
        compiler_params=pltpu.CompilerParams(collective_id=0, has_side_effects=True, vmem_limit_bytes=66_000_000),
        name="correlate",
    )(src_block, raw, quality, jnp.asarray(low), jnp.asarray(high), jnp.asarray(swap_matrix()))
    tiles = tiles.reshape(16, STEPS, 4, 4, 8, LANES)
    return tiles.transpose(0, 1, 2, 4, 3, 5).reshape(16, STEPS, 32, LAG)


def solution(mesh):
    return jax.shard_map(
        per_device,
        mesh=mesh,
        in_specs=(P("tm", "chan", None, None), P(), P("chan")),
        out_specs=P("tm", None, "chan", None),
        check_vma=False,
    )
```

```python
import math

import jax
import jax.numpy as jnp
import numpy as np
from jax import lax
from jax.experimental import pallas as pl
from jax.experimental.pallas import tpu as pltpu
from jax.sharding import PartitionSpec as P

LAG = 512
STEPS = 2
WINDOWS = 16
BINS, LANES, FINE = 2048, 128, 256
HALF_ROWS = LAG // 2 + 16

MESH = pl.DeviceIdType.MESH
GROUP = 16


def pair_even(i):
    return i + 1 - 2 * (i % 2)


def pair_odd(i, n):
    return (i + 2 * (i % 2) - 1 + n) % n


def half_even(i):
    return ((i + 1) // 2) % 2


def half_odd(i):
    return i // 2


def coords(chan):
    return chan // 16, (chan // 4) % 4, (chan // 2) % 2, chan % 2


def chan_of(z, x, y, core):
    return ((z * 4 + x) * 2 + y) * 2 + core


def angle_tables():
    scale = 1.0 / math.sqrt(2.0 * BINS * WINDOWS)
    bins = np.arange(BINS, dtype=np.int64)[None, :]
    low = np.arange(8, dtype=np.int64)[:, None] * bins % (2 * BINS) * (math.pi / BINS)
    high = np.arange(0, HALF_ROWS, 8, dtype=np.int64)[:, None] * bins % (2 * BINS) * (math.pi / BINS)
    f32 = np.float32
    return (np.stack([np.cos(low), np.sin(low)]) * scale).astype(f32), np.stack([np.cos(high), np.sin(high)]).astype(f32)


def swap_matrix():
    lane = np.arange(LANES)
    swap = np.zeros((LANES, LANES), np.float32)
    imag = lane // 8 % 2
    swap[lane ^ 8, lane] = np.where(imag == 0, 1.0, -1.0)
    return swap.astype(jnp.bfloat16)


def kernel(
    blk_ref, raw_ref, quality_ref, low_ref, high_ref, swap_ref, out_ref,
    own, r1, cur1, rc, cur2, r2, cur3, rm00, rm01, rm10, rm11, src,
    swapped, table, cross, rhs, kept, outgoing, incoming, *sems,
):
    s1s, s1r, scs, scr, s2s, s2r, sms, smr, gms, gmr, g2s, g2r, g1s, g1r, gcs, gcr, xs, xr = sems
    f32, bf16 = jnp.float32, jnp.bfloat16
    tm = lax.axis_index("tm")
    z, x, y, core = coords(lax.axis_index("chan"))
    z_even, z_odd = pair_even(z), pair_odd(z, 8)
    x_even, x_odd = pair_even(x), pair_odd(x, 4)
    z_half = z % 2
    at_xe, at_xo = chan_of(z, x_even, y, core), chan_of(z, x_odd, y, core)
    at_ze, at_zo = chan_of(z_even, x, y, core), chan_of(z_odd, x, y, core)
    at_core = chan_of(z, x, y, 1 - core)
    parts = [
        (at_xe, at_ze, half_even(x), z_half),
        (at_ze, at_xe, z_half, half_even(x)),
        (at_xo, at_zo, half_odd(x), z_half),
        (at_zo, at_xo, z_half, half_odd(x)),
    ]
    mine = [half_odd(x) * 8 + y * 4 + z // 2, half_even(x) * 8 + y * 4 + z // 2]
    peers = [[], []]
    for pair in range(2):
        for offset in range(1, GROUP):
            d_x, d_y, d_z = offset // 8, (offset // 4) % 2, offset % 4
            far_x = (x_odd, x_even)[pair] if d_x else x
            peer_z = z_half + 2 * ((z // 2 + d_z) % 4)
            peer_y = (y + d_y) % 2
            half = (half_odd(far_x), half_even(far_x))[pair]
            peers[pair].append((chan_of(peer_z, far_x, peer_y, core), half * 8 + peer_y * 4 + peer_z // 2))

    barrier = pltpu.get_barrier_semaphore()
    greet = [at_ze, at_zo, at_core] + [c for c, _ in peers[0]] + [c for c, _ in peers[1][7:]]
    for to in greet:
        pl.semaphore_signal(barrier, inc=1, device_id={"chan": to}, device_id_type=MESH)
    pl.semaphore_signal(barrier, inc=1, device_id={"tm": 1 - tm}, device_id_type=MESH)

    @pl.loop(0, 8)
    def _(i):
        for u in range(4):
            c = 4 * i + u
            value = raw_ref[:, c].astype(f32).reshape(LANES, FINE).T * quality_ref[c].astype(f32)
            for p in range(4):
                cross[p // 2, p % 2, pl.ds(c, 64, stride=32), :] = value[64 * p : 64 * p + 64]

    def add_power(i, total):
        for p in range(4):
            for u in range(4):
                v = cross[p // 2, p % 2, pl.ds(pl.multiple_of(i * 128 + u * 32, 32), 32), :]
                total = total + v * v
        return total

    power = lax.fori_loop(0, 16, add_power, jnp.zeros((32, LANES), f32))
    lane1 = lax.broadcasted_iota(jnp.int32, (32, LANES), 1)
    for shift in (1, 2, 4, 8):
        other = jnp.where(lane1 // shift % 2 == 0, pltpu.roll(power, LANES - shift, 1), pltpu.roll(power, shift, 1))
        power = power + other
    scale = 1.0 / jnp.sqrt(power / (2.0 * BINS) + 1e-06)
    for p in range(4):

        @pl.loop(0, 8)
        def _(i):
            for u in range(8):
                v = cross[p // 2, p % 2, pl.ds(pl.multiple_of(i * 256 + u * 32, 32), 32), :] * scale
                for j in range(2):
                    own[p, i // 4, i // 2 % 2, i % 2, 2 * u + j] = v[16 * j : 16 * j + 16].astype(bf16)

    pl.semaphore_wait(barrier, len(greet) + 1)

    roots = [coords(blk_ref[k]) for k in range(STEPS)]
    from_xe = [r[1] == x_even for r in roots]
    from_xo = [r[1] == x_odd for r in roots]
    from_ze = [r[0] == z_even for r in roots]
    from_zo = [r[0] == z_odd for r in roots]
    from_core = [r[3] != core for r in roots]
    first_from = [from_xe, from_ze, from_xo, from_zo]
    second_from = [from_ze, from_xe, from_zo, from_xo]
    chosen = []
    for pair in range(2):
        row = []
        for r in roots:
            if pair == 0:
                row.append(half_odd(r[1]) * 8 + r[2] * 4 + r[0] // 2)
            else:
                z_in = jnp.where(r[0] % 2 == z_half, r[0] // 2, pair_odd(r[0], 8) // 2)
                row.append(half_even(r[1]) * 8 + r[2] * 4 + z_in)
        chosen.append(row)
    rm = ((rm00, rm01), (rm10, rm11))

    def send(src_ref, dst_ref, ssem, rsem, to):
        copy = pltpu.make_async_remote_copy(
            src_ref=src_ref, dst_ref=dst_ref, send_sem=ssem, recv_sem=rsem,
            device_id={"chan": to}, device_id_type=MESH,
        )
        copy.start()
        return copy

    first = []
    for p, (to, _, b1, _) in enumerate(parts):
        first.append(send(own.at[p, :, 1 - b1], r1.at[p], s1s.at[p], s1r.at[p], to))

    @pl.loop(0, HALF_ROWS // 16)
    def _(i):
        for part in range(BINS // 512):
            lanes = pl.ds(part * 512, 512)
            lc, ls = low_ref[0, :, lanes], low_ref[1, :, lanes]
            cos, sin = [], []
            for h in range(2):
                hc, hs = high_ref[0, pl.ds(2 * i + h, 1), lanes], high_ref[1, pl.ds(2 * i + h, 1), lanes]
                cos.append(lc * hc - ls * hs)
                sin.append(-(ls * hc + lc * hs))
            rows = pl.ds(pl.multiple_of(i * 16, 16), 16)
            table[rows, lanes] = jnp.concatenate(cos, 0).astype(bf16)
            table[rows, pl.ds(BINS + part * 512, 512)] = jnp.concatenate(sin, 0).astype(bf16)

    for p in range(4):

        @pl.loop(0, 8)
        def _(i):
            chunk = own[p, i // 4, i // 2 % 2, i % 2].reshape(256, LANES)
            swapped[8 * p + i] = (
                jnp.dot(chunk, swap_ref[...], preferred_element_type=f32).astype(bf16).reshape(GROUP, 16, LANES)
            )

    cores, second, group, gather, back2, back1, backc = ([[None] * 4 for _ in range(STEPS)] for _ in range(7))

    def start_core_stage(p):
        _, _, b1, _ = parts[p]
        first[p].wait_recv()

        @pl.loop(0, GROUP)
        def _(m):
            held, got = own[p, :, b1, :, m], r1[p, :, :, m]
            for k in range(STEPS):
                cur1[k, p, :, :, m] = jnp.where(first_from[p][k], got, held)

        for k in range(STEPS):
            cores[k][p] = send(cur1.at[k, p, 1 - core], rc.at[k, p], scs.at[k, p], scr.at[k, p], at_core)

    def start_second(k, p):
        _, to, _, b2 = parts[p]
        cores[k][p].wait_recv()

        @pl.loop(0, GROUP)
        def _(m):
            cur2[k, p, :, m] = jnp.where(from_core[k], rc[k, p, :, m], cur1[k, p, core, :, m])

        second[k][p] = send(cur2.at[k, p, 1 - b2], r2.at[k, p], s2s.at[k, p], s2r.at[k, p], to)

    def take_second(k, p):
        b2 = parts[p][3]
        second[k][p].wait_recv()

        @pl.loop(0, GROUP)
        def _(m):
            cur3[p // 2, p % 2, k, m] = jnp.where(second_from[p][k], r2[k, p, m], cur2[k, p, b2, m])

    def start_group(k):
        for pair in range(2):
            at = mine[pair]
            group[k][pair] = [
                send(cur3.at[pair, :, k, slot], rm[pair][k].at[at], sms.at[k, pair, j], smr.at[k, pair, j], to)
                for j, (to, slot) in enumerate(peers[pair])
            ]
            rm[pair][k][at] = cur3[pair, :, k, at]

    def spot(k, p, level):
        _, _, b1, b2 = parts[p]
        if level == 0:
            return src.at[k, pl.ds((((p * 2 + core) * 2 + b1) * 2 + b2) * 16 + mine[p // 2], 1)]
        if level == 1:
            return src.at[k, pl.ds((((p * 2 + core) * 2 + b1) * 2 + b2) * 16, 16)]
        if level == 2:
            return src.at[k, pl.ds(((p * 2 + core) * 2 + b1) * 32, 32)]
        return src.at[k, pl.ds((p * 2 + core) * 64, 64)]

    def start_gather(k):
        for pair in range(2):
            for copy in group[k][pair]:
                copy.wait_recv()
            for p in (2 * pair, 2 * pair + 1):
                _, _, b1, b2 = parts[p]
                at = (((p * 2 + core) * 2 + b1) * 2 + b2) * 16 + mine[pair]
                src[k, at] = rm[pair][k][chosen[pair][k], p % 2]
                gather[k][p] = [
                    send(spot(k, p, 0), spot(k, p, 0), gms.at[k, p, j], gmr.at[k, p, j], to)
                    for j, (to, _) in enumerate(peers[pair])
                ]

    def start_back2(k):
        for p in range(4):
            for copy in gather[k][p]:
                copy.wait_recv()
            back2[k][p] = send(spot(k, p, 1), spot(k, p, 1), g2s.at[k, p], g2r.at[k, p], parts[p][1])

    def start_back1(k):
        for p in range(4):
            back2[k][p].wait_recv()
            back1[k][p] = send(spot(k, p, 2), spot(k, p, 2), g1s.at[k, p], g1r.at[k, p], parts[p][0])

    def start_core(k):
        for p in range(4):
            back1[k][p].wait_recv()
            backc[k][p] = send(spot(k, p, 3), spot(k, p, 3), gcs.at[k, p], gcr.at[k, p], at_core)

    lane2 = lax.broadcasted_iota(jnp.int32, (1, 2 * LANES), 1)
    lane0 = lax.broadcasted_iota(jnp.int32, (1, LANES), 1)
    fmask = [(lane2 % 4 == f4).astype(f32).astype(bf16) for f4 in range(4)]
    qmask = [(lane0 // 4 % 2 == q).astype(f32).astype(bf16) for q in range(2)]
    zero = jnp.zeros((32, LANES), bf16)
    low_lane = lax.broadcasted_iota(jnp.int32, (8, LANES), 1) < 64

    def products(k, p):
        backc[k][p].wait_recv()

        @pl.loop(0, 4)
        def _(half_i):
            for uu in range(16):
                i, u = half_i * 2 + uu // 8, uu % 8
                real = [own[p, half_i // 2, half_i % 2, uu // 8, 2 * u + j] for j in range(2)]
                imag = [swapped[8 * p + i, 2 * u + j] for j in range(2)]
                pieces = [jnp.concatenate(v, 1) for v in (real, imag)]
                lhs = jnp.concatenate([v * fmask[f4] for f4 in range(4) for v in pieces], 0)
                at = p * 128 + i * 16 + 2 * u
                sources = jnp.concatenate([src[k, at + h] for h in (tm, 1 - tm)], 0)
                rows = []
                for q in range(2):
                    masked = sources * qmask[q]
                    rows += [jnp.concatenate([masked, zero], 1), jnp.concatenate([zero, masked], 1)]
                weights = jnp.concatenate(rows, 0)
                product = lax.dot_general(lhs, weights, (((1,), (1,)), ((), ())), preferred_element_type=f32)
                row = pl.multiple_of((p * 64 + i * 8 + u) * 8, 8)
                for n in range(8):
                    upper, lower = product[16 * n : 16 * n + 8], product[16 * n + 8 : 16 * n + 16]
                    cross[n, 0, pl.ds(row, 8), :] = jnp.where(low_lane, upper, pltpu.roll(lower, 64, 1))
                    cross[n, 1, pl.ds(row, 8), :] = jnp.where(low_lane, pltpu.roll(upper, 64, 1), lower)

    def transfer(at):
        return pltpu.make_async_remote_copy(
            src_ref=outgoing.at[at], dst_ref=incoming.at[at], send_sem=xs.at[at], recv_sem=xr.at[at],
            device_id={"tm": 1 - tm}, device_id_type=MESH,
        )

    lane3 = lax.broadcasted_iota(jnp.int32, (FINE, LANES), 1)
    lane_zero, mirrored = lane3 == 0, (LANES - lane3) % LANES

    def mirror(value):
        return jnp.take_along_axis(value, mirrored, axis=1, mode="promise_in_bounds")

    def lags(k):
        @pl.loop(0, 4)
        def _(cols):
            for q in range(2):
                for f4 in range(4):
                    for ri in range(2):
                        for half in range(2):
                            value = cross[f4 * 2 + ri, q, pl.ds(2 * cols + half, FINE, stride=8), :]
                            rows = pl.ds(ri * BINS + (q * 4 + f4) * FINE, FINE)
                            rhs[rows, pl.ds(half * LANES, LANES)] = value.astype(bf16)
            even = jnp.dot(table[:, :BINS], rhs[:BINS], preferred_element_type=f32)
            odd = jnp.dot(table[:, BINS:], rhs[BINS:], preferred_element_type=f32)
            right, left = (even + odd)[:FINE].T, (even - odd)[:FINE].T
            farthest = (even - odd)[FINE : FINE + 8].T[:, :1]
            near, far = (mirror(left[:, at : at + LANES]) for at in (0, LANES))
            sums = jnp.concatenate([jnp.where(lane_zero, farthest, far), jnp.where(lane_zero, far, near), right], 1)
            at = k * 4 + cols
            for n in range(8):
                kept[at, pl.ds(n * 16, 16)] = sums[n * 32 : n * 32 + 16]
                outgoing[at, pl.ds(n * 16, 16)] = sums[n * 32 + 16 : n * 32 + 32].astype(bf16)
            transfer(at).start()

    def finish(k):
        @pl.loop(0, 4)
        def _(cols):
            at = k * 4 + cols
            transfer(at).wait_recv()
            for half in range(2):
                for h in range(2):
                    for j in range(2):
                        spot16 = pl.ds(((half * 2 + h) * 2 + j) * 16, 16)
                        total = kept[at, spot16] + incoming[at, spot16].astype(f32)
                        channel = 2 * cols + half
                        for part in range(4):
                            row = k * 128 + (j * 2 + h) * 32 + part * 8 + channel
                            out_ref[pl.ds(row, 16, stride=256), :] = total[:, part * LANES : (part + 1) * LANES]

    for p in range(4):
        start_core_stage(p)
    for p in range(4):
        start_second(0, p)
    for p in range(4):
        take_second(0, p)
    start_group(0)
    for p in range(4):
        start_second(1, p)
    for p in range(4):
        take_second(1, p)
    start_gather(0)
    start_group(1)
    start_back2(0)
    start_back1(0)
    start_gather(1)
    start_core(0)
    products(0, 0)
    start_back2(1)
    products(0, 1)
    start_back1(1)
    products(0, 2)
    start_core(1)
    products(0, 3)
    lags(0)
    for p in range(4):
        products(1, p)
    lags(1)
    finish(0)
    finish(1)

    @pl.loop(0, 8)
    def _(at):
        transfer(at).wait_send()

    for copy in first:
        copy.wait_send()
    for k in range(STEPS):
        for copy in cores[k] + second[k] + back2[k] + back1[k] + backc[k] + sum(gather[k], []) + group[k][0] + group[k][1]:
            copy.wait_send()


def per_device(spectra, src_block, quality):
    f32, bf16 = jnp.float32, jnp.bfloat16
    raw = spectra
    low, high = angle_tables()
    vmem, smem = (pl.BlockSpec(memory_space=space) for space in (pltpu.VMEM, pltpu.SMEM))
    dma = pltpu.SemaphoreType.DMA
    rows = lambda *s: pltpu.VMEM(s + (16, LANES), bf16)
    sems = []
    for shape in ((4,), (2, 4), (2, 4), (2, 2, 15), (2, 4, 15), (2, 4), (2, 4), (2, 4), (8,)):
        sems += [dma(shape), dma(shape)]
    tiles = pl.pallas_call(
        kernel,
        out_shape=jax.ShapeDtypeStruct((16 * STEPS * 32 * 4, LANES), f32),
        in_specs=[smem, vmem, smem] + [vmem] * 3,
        out_specs=vmem,
        scratch_shapes=[
            rows(4, 2, 2, 2, GROUP),
            rows(4, 2, 2, GROUP),
            rows(STEPS, 4, 2, 2, GROUP),
            rows(STEPS, 4, 2, GROUP),
            rows(STEPS, 4, 2, GROUP),
            rows(STEPS, 4, GROUP),
            rows(2, 2, STEPS, GROUP),
            rows(GROUP, 2),
            rows(GROUP, 2),
            rows(GROUP, 2),
            rows(GROUP, 2),
            rows(STEPS, 512),
            rows(32, GROUP),
            pltpu.VMEM((HALF_ROWS, 2 * BINS), bf16),
            pltpu.VMEM((8, 2, FINE * 8, LANES), f32),
            pltpu.VMEM((2 * BINS, 2 * LANES), bf16),
            pltpu.VMEM((8, LANES, LAG), f32),
            pltpu.VMEM((8, LANES, LAG), bf16),
            pltpu.VMEM((8, LANES, LAG), bf16),
        ]
        + sems,
        compiler_params=pltpu.CompilerParams(collective_id=0, has_side_effects=True, vmem_limit_bytes=66_000_000),
        name="correlate",
    )(src_block, raw, quality, jnp.asarray(low), jnp.asarray(high), jnp.asarray(swap_matrix()))
    tiles = tiles.reshape(16, STEPS, 4, 4, 8, LANES)
    return tiles.transpose(0, 1, 2, 4, 3, 5).reshape(16, STEPS, 32, LAG)


def solution(mesh):
    return jax.shard_map(
        per_device,
        mesh=mesh,
        in_specs=(P("tm", "chan", None, None), P(), P("chan")),
        out_specs=P("tm", None, "chan", None),
        check_vma=False,
    )
```
